512 devices in a mesh: dp: 32 (over x_hi, z), tm: 16 (over y, x_lo, core).
Axes of the slice: x: 4 (x_hi: 2, x_lo: 2; x = x_hi * 2 + x_lo), y: 4, z: 16, core: 2. Of those that a mesh axis runs over, the one named last changes fastest.
Arguments:
- clip_input: bfloat16 [32, 32, 256, 384], P('dp', 'tm'), may hold values from -32 to 32
- norm_gain: float32 [384], replicated, may hold values from 0.1 to 1.9
- qkv_weight: bfloat16 [384, 1152], replicated, may hold values from -2 to 2
- out_weight: bfloat16 [384, 384], replicated, may hold values from -0.3125 to 0.3125
- time_weight: bfloat16 [3, 384, 768], P(None, 'dp'), may hold values from -0.1875 to 0.1875
- upsample_cotangent: bfloat16 [32, 32, 256, 768], P('dp', 'tm'), may hold values from -6 to 6
Outputs:
- input_grad: bfloat16 [32, 32, 256, 384], P('dp', 'tm')
- qkv_grad: float32 [384, 1152], P('dp', 'tm')
The draws below stay inside these ranges and needn't reach their ends.
All inputs are finite; a program needn't handle non-finite values.
Results may differ from the reference program's by a relative error of at most 0.024.
Values may be sent and summed in bfloat16 or wider, within the bound.
No kernel may reach another device: no remote copies, remote signals or barrier semaphores. Data moves between devices by JAX's collectives and lax.ppermute only.
A program may use at most 64 MiB of HBM per device.

```python
import math
import jax
import jax.numpy as jnp
from jax import lax

C = 384
HW = 256
FRAMES = 32
CLIPS = 32
WIDE = 768


def draw_clip_input(key, part):
    own_key = jax.random.fold_in(key, 11)
    pair_key, jitter_key = jax.random.split(own_key, 2)
    block_width = C // CLIPS
    pairing = jax.random.permutation(pair_key, CLIPS)
    channel_block = jnp.arange(C) // block_width
    spiked = 1.0 + 3.0 * (channel_block[None, :] == pairing[:, None]).astype(jnp.float32)
    jitter = jax.random.truncated_normal(jitter_key, -6.0, 6.0, (CLIPS, FRAMES, HW, C), jnp.float32)
    values = jitter * spiked[:, None, None, :]
    return values.astype(jnp.bfloat16)


def draw_qkv_weight(key, part):
    own_key = jax.random.fold_in(key, 23)
    random_key = jax.random.fold_in(own_key, 0)
    spread = C ** (-0.5)
    values = jax.random.truncated_normal(random_key, -6.0, 6.0, (C, 3 * C), jnp.float32) * spread
    return values.astype(jnp.bfloat16)


def steps_of(rng, extent, cuts, least, largest):
    level = 1.0
    for dim, blocks in cuts:
        steps = jax.random.uniform(jax.random.fold_in(jax.random.fold_in(rng, 6), dim), (blocks,), jnp.float32, least / len(cuts), largest / len(cuts))
        level = level * jnp.repeat(jnp.exp(steps), extent[dim] // blocks).reshape((-1,) + (1,) * (len(extent) - 1 - dim))
    return level


def scatter_about(key, shape, scale, bound, cuts=(), held_as=jnp.bfloat16):
    entries = scale * jax.random.normal(key, shape, jnp.float32)
    if cuts:
        entries = entries * steps_of(key, shape, cuts, -0.22, 0.18)
    return jnp.clip(entries, -bound, bound).astype(held_as)


def setup_inputs(seed: int = 0) -> dict:
    key_of = jax.random.split(jax.random.key(seed), 7)
    clip_input = draw_clip_input(jax.random.fold_in(key_of[6], 71), 0)
    norm_gain = jnp.clip(1.0 + 0.18 * jax.random.normal(key_of[1], (C,), jnp.float32), 0.1, 1.9)
    qkv_weight = draw_qkv_weight(jax.random.fold_in(key_of[6], 71), 0)
    out_weight = scatter_about(key_of[3], (C, C), C ** -0.5, 0.3125)
    time_weight = scatter_about(key_of[4], (3, C, WIDE), (3 * C) ** -0.5, 0.1875, ((1, 32),))
    upsample_cotangent = scatter_about(key_of[5], (CLIPS, FRAMES, HW, WIDE), 1.0, 6.0, ((0, 32), (1, 16)))
    return {"clip_input": clip_input, "norm_gain": norm_gain, "qkv_weight": qkv_weight, "out_weight": out_weight, "time_weight": time_weight, "upsample_cotangent": upsample_cotangent}


def rms_scaled(features, norm_gain):
    squares = lax.optimization_barrier(jnp.mean(features * features, axis=-1, keepdims=True))
    return features * lax.rsqrt(squares + 1e-06) * norm_gain

def block_tail(qkv_rows, features, out_weight):
    width = features.shape[-1]
    queries = qkv_rows[..., :width]
    keys = qkv_rows[..., width:2 * width]
    values = qkv_rows[..., 2 * width:]
    scores = jnp.einsum('fqc,fkc->fqk', queries, keys, preferred_element_type=jnp.float32) / math.sqrt(width)
    weights = jax.nn.softmax(scores, axis=-1).astype(jnp.bfloat16)
    mixed = jnp.einsum('fqk,fkc->fqc', weights, values, preferred_element_type=jnp.float32).astype(jnp.bfloat16)
    branch = jnp.einsum('fqc,cd->fqd', mixed, out_weight, preferred_element_type=jnp.float32)
    return (features + branch).astype(jnp.bfloat16)

def attention_grads(clip_rows, norm_gain, qkv_weight, out_weight, upstream):
    features = clip_rows.astype(jnp.float32)
    normed, pre_back = jax.vjp(lambda value: rms_scaled(value, norm_gain), features)
    normed_bf = normed.astype(jnp.bfloat16)
    qkv_rows = jnp.einsum('fhc,cd->fhd', normed_bf, qkv_weight, preferred_element_type=jnp.float32).astype(jnp.bfloat16)
    block_out, tail_back = jax.vjp(lambda first, second: block_tail(first, second, out_weight), qkv_rows, features)
    qkv_cot, feature_cot = tail_back(upstream)
    normed_cot = jnp.einsum('fhd,cd->fhc', qkv_cot, qkv_weight, preferred_element_type=jnp.float32)
    direct = pre_back(normed_cot)[0]
    input_grad = (feature_cot + direct).astype(jnp.bfloat16)
    return (input_grad, normed_bf, qkv_cot)

def reference(clip_input, norm_gain, qkv_weight, out_weight, time_weight, upsample_cotangent):

    def per_clip(total, pair):
        rows, cotangent = pair
        frames = cotangent.shape[0]
        padded = jnp.concatenate([cotangent, jnp.zeros((2,) + cotangent.shape[1:], cotangent.dtype)], 0)
        upstream = jnp.zeros(rows.shape, jnp.float32)
        for tap in range(3):
            upstream = upstream + jnp.einsum('fhd,cd->fhc', padded[2 - tap:2 - tap + frames], time_weight[tap], preferred_element_type=jnp.float32)
        upstream = upstream.astype(jnp.bfloat16)
        input_grad, normed_bf, qkv_cot = attention_grads(rows, norm_gain, qkv_weight, out_weight, upstream)
        term = jnp.einsum('fhc,fhd->cd', normed_bf, qkv_cot, preferred_element_type=jnp.float32)
        return (total + term, input_grad)
    width = clip_input.shape[-1]
    start = jnp.zeros((width, 3 * width), jnp.float32)
    total, grads = lax.scan(per_clip, start, (clip_input, upsample_cotangent))
    return (grads, total)
```

```python
import math

import jax
import jax.numpy as jnp
from jax import lax
from jax.sharding import Mesh
from jax.sharding import PartitionSpec as P

AXES = ("xh", "z", "y", "xl", "co")
SIZES = (2, 16, 4, 2, 2)
DP = ("xh", "z")
TM = ("y", "xl", "co")
PLANE = ("xh", "y", "xl")
PIECES = 8
TILES = 7


def rms_scaled(features, norm_gain):
    squares = jnp.mean(features * features, axis=-1, keepdims=True)
    return features * lax.rsqrt(squares + 1e-06) * norm_gain


def block_tail(qkv_rows, features, out_weight):
    width = features.shape[-1]
    queries = qkv_rows[..., :width]
    keys = qkv_rows[..., width : 2 * width]
    values = qkv_rows[..., 2 * width :]
    scores = jnp.einsum(
        "fqc,fkc->fqk", queries, keys, preferred_element_type=jnp.float32
    ) / math.sqrt(width)
    weights = jax.nn.softmax(scores, axis=-1).astype(jnp.bfloat16)
    mixed = jnp.einsum("fqk,fkc->fqc", weights, values, preferred_element_type=jnp.float32).astype(
        jnp.bfloat16
    )
    branch = jnp.einsum("fqc,cd->fqd", mixed, out_weight, preferred_element_type=jnp.float32)
    return (features + branch).astype(jnp.bfloat16)


def attention_grads(clip_rows, norm_gain, qkv_weight, out_weight, upstream):
    features = clip_rows.astype(jnp.float32)
    normed, pre_back = jax.vjp(lambda value: rms_scaled(value, norm_gain), features)
    normed_bf = normed.astype(jnp.bfloat16)
    qkv_rows = jnp.einsum(
        "fhc,cd->fhd", normed_bf, qkv_weight, preferred_element_type=jnp.float32
    ).astype(jnp.bfloat16)
    block_out, tail_back = jax.vjp(
        lambda first, second: block_tail(first, second, out_weight), qkv_rows, features
    )
    qkv_cot, feature_cot = tail_back(upstream)
    normed_cot = jnp.einsum("fhd,cd->fhc", qkv_cot, qkv_weight, preferred_element_type=jnp.float32)
    direct = pre_back(normed_cot)[0]
    input_grad = (feature_cot + direct).astype(jnp.bfloat16)
    return (input_grad, normed_bf, qkv_cot)


def spread(block, axes):
    count = math.prod(lax.axis_size(a) for a in axes)
    return lax.all_to_all(
        jnp.broadcast_to(block[None], (count,) + block.shape), axes, 0, 0, tiled=True
    )


def gathered_taps(shard):
    taps, held, wide = shard.shape
    rows, lanes = held // 4, wide // 128
    tiles = shard.reshape(taps, rows, 4, lanes, 128).transpose(0, 3, 1, 2, 4)
    count = taps * lanes * rows
    tiles = tiles.reshape(count, 4, 128)
    tiles = jnp.concatenate([tiles, jnp.zeros((PIECES * TILES - count, 4, 128), tiles.dtype)], 0)
    tiles = tiles.reshape(PIECES, TILES, 4, 128)
    place = lax.axis_index("y") * lax.axis_size("xl") + lax.axis_index("xl")
    mine = lax.dynamic_index_in_dim(tiles, place, 0, keepdims=False)
    column = spread(mine, ("z",))
    half = lax.axis_size("z") // 2
    core = lax.axis_index("co")
    part = lax.dynamic_slice_in_dim(column, core * half, half, 0)
    own = spread(part, PLANE)
    other = lax.ppermute(own, "co", [(0, 1), (1, 0)])
    low = jnp.where(core == 0, own, other)
    high = jnp.where(core == 0, other, own)
    both = jnp.stack([low, high]).reshape(2, lax.axis_size("xh"), PIECES, half, TILES, 4, 128)
    both = both.transpose(1, 0, 3, 2, 4, 5, 6).reshape(-1, PIECES * TILES, 4, 128)[:, :count]
    both = both.reshape(-1, taps, lanes, rows, 4, 128).transpose(1, 0, 3, 4, 2, 5)
    return both.reshape(taps, -1, wide)


def on_device(clip_input, norm_gain, qkv_weight, out_weight, time_weight, upsample_cotangent):
    rows = clip_input[0]
    cotangent = upsample_cotangent[0]
    frames = cotangent.shape[0]
    width = rows.shape[-1]
    slabs = math.prod(lax.axis_size(a) for a in TM)
    clips = math.prod(lax.axis_size(a) for a in DP)
    incoming = lax.ppermute(cotangent, TM, [(i + 1, i) for i in range(slabs - 1)])
    padded = jnp.concatenate([cotangent, incoming], 0)
    piece = gathered_taps(time_weight)
    result = jnp.einsum(
        "fhd,cd->fhc", padded[2 : 2 + frames], piece[0], preferred_element_type=jnp.float32
    )
    result = result + jnp.einsum(
        "fhd,cd->fhc", padded[1 : 1 + frames], piece[1], preferred_element_type=jnp.float32
    )
    upstream = (
        result
        + jnp.einsum("fhd,cd->fhc", padded[0:frames], piece[2], preferred_element_type=jnp.float32)
    ).astype(jnp.bfloat16)
    input_grad, normed_bf, qkv_cot = attention_grads(
        rows, norm_gain, qkv_weight, out_weight, upstream
    )
    flat_normed = normed_bf.reshape(-1, width)
    flat_cot = qkv_cot.reshape(-1, 3 * width)
    share = jnp.einsum("rd,rc->dc", flat_cot, flat_normed, preferred_element_type=jnp.float32)
    share = share.astype(jnp.bfloat16).reshape(slabs, -1, width)
    share = lax.all_to_all(share, TM, 0, 0, tiled=True)
    share = jnp.sum(share.astype(jnp.float32), axis=0).astype(jnp.bfloat16)
    share = share.T.reshape(clips, width // clips, -1)
    share = lax.all_to_all(share, DP, 0, 0, tiled=True)
    qkv_grad = jnp.sum(share.astype(jnp.float32), axis=0)
    return (input_grad[None], qkv_grad)


def solution(mesh):
    split = Mesh(mesh.devices.reshape(SIZES), AXES)
    in_specs = (
        P(DP, TM, None, None),
        P(),
        P(),
        P(),
        P(None, DP, None),
        P(DP, TM, None, None),
    )
    out_specs = (P(DP, TM, None, None), P(DP, TM))
    return jax.shard_map(
        on_device, mesh=split, in_specs=in_specs, out_specs=out_specs, check_vma=False
    )
```

```python
import math

import jax
import jax.numpy as jnp
from jax import lax
from jax.experimental import pallas as pl
from jax.experimental.pallas import tpu as pltpu
from jax.sharding import Mesh
from jax.sharding import PartitionSpec as P

AXES = ("xh", "z", "y", "xl", "co")
SIZES = (2, 16, 4, 2, 2)
DP = ("xh", "z")
TM = ("y", "xl", "co")
PLANE = ("xh", "y", "xl")
PIECES = 8
TILES = 7
LANES = 128
bf16, f32 = jnp.bfloat16, jnp.float32


def dot(a, b, contract):
    return lax.dot_general(a, b, (contract, ((), ())), preferred_element_type=f32)


NN, NT, TN = ((1,), (0,)), ((1,), (1,)), ((0,), (0,))


def forward_kernel(clip_ref, gain_ref, weight_ref, normed_ref, qkv_ref, prob_ref):
    frames, positions, width = clip_ref.shape
    for f in range(frames):
        features = clip_ref[f].astype(f32)
        squares = jnp.mean(features * features, axis=-1, keepdims=True)
        normed = (features * lax.rsqrt(squares + 1e-06) * gain_ref[...]).astype(bf16)
        normed_ref[f] = normed
        qkv = dot(normed, weight_ref[...], NN).astype(bf16)
        qkv_ref[f] = qkv
        scores = dot(qkv[:, :width], qkv[:, width : 2 * width], NT) / math.sqrt(width)
        raised = jnp.exp(scores - jnp.max(scores, axis=-1, keepdims=True))
        prob_ref[f] = raised / jnp.sum(raised, axis=-1, keepdims=True)


def backward_kernel(
    cot_ref, next_ref, own_ref, other_ref, order_ref, out_weight_ref, qkv_ref, prob_ref,
    normed_ref, upstream_ref, qkv_cot_ref, grad_ref, taps_ref,
):
    frames, positions, width = upstream_ref.shape
    rows = frames * positions
    wide = cot_ref.shape[-1]
    taps = taps_ref.shape[0]
    block = own_ref.shape[2]
    groups = own_ref.shape[0] // PIECES
    lanes = wide // LANES
    parts = width // (2 * groups * block)
    for half, source in enumerate((own_ref, other_ref)):
        for group in range(groups):
            for tile in range(taps * lanes * parts):
                tap, rest = divmod(tile, lanes * parts)
                lane, part = divmod(rest, parts)
                start = ((half * groups + group) * parts + part) * block
                taps_ref[tap, start : start + block, lane * LANES : (lane + 1) * LANES] = source[
                    group * PIECES + tile // TILES, tile % TILES
                ]
    middle = jnp.concatenate([cot_ref[1], next_ref[0]], axis=0)
    total = dot(cot_ref[...].reshape(rows, wide), taps_ref[2], NT)
    total = total + dot(middle, taps_ref[1], NT)
    total = total + dot(next_ref[...].reshape(rows, wide), taps_ref[0], NT)
    upstream = dot(total.astype(bf16), order_ref[...], NN).astype(bf16)
    upstream_ref[...] = upstream.reshape(upstream_ref.shape)
    mixed_cot = dot(upstream, out_weight_ref[...], NT).astype(bf16)
    for f in range(frames):
        cot = mixed_cot[f * positions : (f + 1) * positions]
        prob = prob_ref[f]
        queries = qkv_ref[f, :, :width]
        keys = qkv_ref[f, :, width : 2 * width]
        values = qkv_ref[f, :, 2 * width :]
        weights_cot = dot(cot, values, NT).astype(bf16).astype(f32)
        pull = jnp.sum(weights_cot * prob, axis=-1, keepdims=True)
        scores_cot = (prob * (weights_cot - pull) / math.sqrt(width)).astype(bf16)
        qkv_cot_ref[f, :, :width] = dot(scores_cot, keys, NN).astype(bf16)
        qkv_cot_ref[f, :, width : 2 * width] = dot(scores_cot, queries, TN).astype(bf16)
        qkv_cot_ref[f, :, 2 * width :] = dot(prob.astype(bf16), cot, TN).astype(bf16)
    grad_ref[...] = dot(
        qkv_cot_ref[...].reshape(rows, 3 * width), normed_ref[...].reshape(rows, width), TN
    ).astype(bf16)


def input_kernel(clip_ref, gain_ref, weight_ref, qkv_cot_ref, upstream_ref, out_ref):
    frames, positions, width = clip_ref.shape
    for f in range(frames):
        features = clip_ref[f].astype(f32)
        squares = jnp.mean(features * features, axis=-1, keepdims=True)
        scale = lax.rsqrt(squares + 1e-06)
        cot = dot(qkv_cot_ref[f], weight_ref[...], NT) * gain_ref[...]
        along = jnp.mean(features * cot, axis=-1, keepdims=True)
        direct = scale * cot - features * (scale * scale * scale * along)
        out_ref[f] = (upstream_ref[f].astype(f32) + direct).astype(bf16)


def whole(count):
    return [pl.BlockSpec(memory_space=pltpu.VMEM)] * count


def call(kernel, outs, args, flops, limit, scratch=()):
    moved = sum(a.size * a.dtype.itemsize for a in args)
    moved += sum(math.prod(s) * jnp.dtype(d).itemsize for s, d in outs)
    return pl.pallas_call(
        kernel,
        out_shape=tuple(jax.ShapeDtypeStruct(s, d) for s, d in outs),
        in_specs=whole(len(args)),
        out_specs=tuple(whole(len(outs))),
        scratch_shapes=list(scratch),
        cost_estimate=pl.CostEstimate(flops=flops, bytes_accessed=moved, transcendentals=0),
        compiler_params=pltpu.CompilerParams(vmem_limit_bytes=limit << 20),
    )(*args)


def spread(block, axes):
    count = math.prod(lax.axis_size(a) for a in axes)
    return lax.all_to_all(
        jnp.broadcast_to(block[None], (count,) + block.shape), axes, 0, 0, tiled=True
    )


def tap_column(shard):
    taps, held, wide = shard.shape
    rows, lanes = held // 4, wide // LANES
    tiles = shard.reshape(taps, rows, 4, lanes, LANES).transpose(0, 3, 1, 2, 4)
    count = taps * lanes * rows
    tiles = tiles.reshape(count, 4, LANES)
    tiles = jnp.concatenate([tiles, jnp.zeros((PIECES * TILES - count, 4, LANES), tiles.dtype)], 0)
    tiles = tiles.reshape(PIECES, TILES, 4, LANES)
    place = lax.axis_index("y") * lax.axis_size("xl") + lax.axis_index("xl")
    column = spread(lax.dynamic_index_in_dim(tiles, place, 0, keepdims=False), ("z",))
    half = lax.axis_size("z") // 2
    part = lax.dynamic_slice_in_dim(column, lax.axis_index("co") * half, half, 0)
    return part.transpose(1, 0, 2, 3).reshape(TILES, half * 4, LANES)


def channel_order(width):
    depth, groups = lax.axis_size("z"), lax.axis_size("xh")
    half = depth // 2
    held = width // (depth * groups)
    parts = held // 4
    place = jnp.arange(width)
    row, place = place % 4, place // 4
    level, place = place % half, place // half
    part, place = place % parts, place // parts
    group, side = place % groups, place // groups
    level = level + half * jnp.where(lax.axis_index("co") == 0, side, 1 - side)
    channel = held * (group * depth + level) + 4 * part + row
    return (channel[:, None] == jnp.arange(width)[None, :]).astype(bf16)


def on_device(clip_input, norm_gain, qkv_weight, out_weight, time_weight, upsample_cotangent):
    clip = clip_input[0]
    cotangent = upsample_cotangent[0]
    frames, positions, width = clip.shape
    wide = cotangent.shape[-1]
    rows = frames * positions
    slabs = math.prod(lax.axis_size(a) for a in TM)
    clips = math.prod(lax.axis_size(a) for a in DP)
    gain = norm_gain[None]

    incoming = lax.ppermute(cotangent, TM, [(i + 1, i) for i in range(slabs - 1)])
    column = tap_column(time_weight)
    normed, qkv, prob = call(
        forward_kernel,
        [((frames, positions, width), bf16), ((frames, positions, 3 * width), bf16),
         ((frames, positions, positions), f32)],
        [clip, gain, qkv_weight],
        2 * rows * width * (3 * width + positions),
        16,
    )
    order = channel_order(width)
    column, incoming, normed, qkv, prob, order = lax.optimization_barrier(
        (column, incoming, normed, qkv, prob, order)
    )
    own = spread(column, PLANE)
    other = lax.ppermute(own, "co", [(0, 1), (1, 0)])
    upstream, qkv_cot, grad = call(
        backward_kernel,
        [((frames, positions, width), bf16), ((frames, positions, 3 * width), bf16),
         ((3 * width, width), bf16)],
        [cotangent, incoming, own, other, order, out_weight, qkv, prob, normed],
        2 * rows * width * (3 * wide + 2 * width + 4 * positions + 3 * width),
        32,
        [pltpu.VMEM((3, width, wide), bf16)],
    )
    share = grad.reshape(slabs, -1, width)
    share = lax.all_to_all(share, TM, 0, 0, tiled=True)
    (input_grad,) = call(
        input_kernel,
        [((frames, positions, width), bf16)],
        [clip, gain, qkv_weight, qkv_cot, upstream],
        2 * rows * width * 3 * width,
        16,
    )
    share = jnp.sum(share.astype(f32), axis=0).astype(bf16)
    share = share.T.reshape(clips, width // clips, -1)
    share = lax.all_to_all(share, DP, 0, 0, tiled=True)
    qkv_grad = jnp.sum(share.astype(f32), axis=0)
    return (input_grad[None], qkv_grad)


def solution(mesh):
    split = Mesh(mesh.devices.reshape(SIZES), AXES)
    in_specs = (
        P(DP, TM, None, None),
        P(),
        P(),
        P(),
        P(None, DP, None),
        P(DP, TM, None, None),
    )
    out_specs = (P(DP, TM, None, None), P(DP, TM))
    return jax.shard_map(
        on_device, mesh=split, in_specs=in_specs, out_specs=out_specs, check_vma=False
    )
```

```python
import math

import jax
import jax.numpy as jnp
from jax import lax
from jax.experimental import pallas as pl
from jax.experimental.pallas import tpu as pltpu
from jax.sharding import Mesh
from jax.sharding import PartitionSpec as P

AXES = ("xh", "z", "y", "xl", "co")
SIZES = (2, 16, 4, 2, 2)
DP = ("xh", "z")
TM = ("y", "xl", "co")
PLANE = ("xh", "y", "xl")
PIECES = 8
TILES = 7
LANES = 128
bf16, f32 = jnp.bfloat16, jnp.float32


def dot(a, b, contract):
    return lax.dot_general(a, b, (contract, ((), ())), preferred_element_type=f32)


NN, NT, TN = ((1,), (0,)), ((1,), (1,)), ((0,), (0,))


def forward_kernel(clip_ref, gain_ref, weight_ref, normed_ref, qkv_ref, prob_ref):
    frames, positions, width = clip_ref.shape
    for f in range(frames):
        features = clip_ref[f].astype(f32)
        squares = jnp.mean(features * features, axis=-1, keepdims=True)
        normed = (features * lax.rsqrt(squares + 1e-06) * gain_ref[...]).astype(bf16)
        normed_ref[f] = normed
        qkv = dot(normed, weight_ref[...], NN).astype(bf16)
        qkv_ref[f] = qkv
        scores = dot(qkv[:, :width], qkv[:, width : 2 * width], NT) / math.sqrt(width)
        raised = jnp.exp(scores - jnp.max(scores, axis=-1, keepdims=True))
        prob_ref[f] = raised / jnp.sum(raised, axis=-1, keepdims=True)


def backward_kernel(
    core_ref, cot_any, next_any, own_ref, other_ref, order_ref, out_weight_ref, qkv_ref, prob_ref,
    normed_ref, upstream_ref, qkv_cot_ref, keep_ref, send_ref, taps_ref, cot_ref, next_ref,
    grad_ref, sems,
):
    frames, positions, width = upstream_ref.shape
    rows = frames * positions
    wide = cot_ref.shape[-1]
    taps = taps_ref.shape[0]
    block = own_ref.shape[2]
    groups = own_ref.shape[0] // PIECES
    lanes = wide // LANES
    parts = width // (2 * groups * block)
    copies = [
        pltpu.make_async_copy(cot_any, cot_ref, sems.at[0]),
        pltpu.make_async_copy(next_any, next_ref, sems.at[1]),
    ]
    for copy in copies:
        copy.start()
    for half, source in enumerate((own_ref, other_ref)):
        for group in range(groups):
            for tile in range(taps * lanes * parts):
                tap, rest = divmod(tile, lanes * parts)
                lane, part = divmod(rest, parts)
                start = ((half * groups + group) * parts + part) * block
                taps_ref[tap, start : start + block, lane * LANES : (lane + 1) * LANES] = source[
                    group * PIECES + tile // TILES, tile % TILES
                ]
    for copy in copies:
        copy.wait()
    middle = jnp.concatenate([cot_ref[1], next_ref[0]], axis=0)
    total = dot(cot_ref[...].reshape(rows, wide), taps_ref[2], NT)
    total = total + dot(middle, taps_ref[1], NT)
    total = total + dot(next_ref[...].reshape(rows, wide), taps_ref[0], NT)
    upstream = dot(total.astype(bf16), order_ref[...], NN).astype(bf16)
    upstream_ref[...] = upstream.reshape(upstream_ref.shape)
    mixed_cot = dot(upstream, out_weight_ref[...], NT).astype(bf16)
    for f in range(frames):
        cot = mixed_cot[f * positions : (f + 1) * positions]
        prob = prob_ref[f]
        queries = qkv_ref[f, :, :width]
        keys = qkv_ref[f, :, width : 2 * width]
        values = qkv_ref[f, :, 2 * width :]
        weights_cot = dot(cot, values, NT).astype(bf16).astype(f32)
        pull = jnp.sum(weights_cot * prob, axis=-1, keepdims=True)
        scores_cot = (prob * (weights_cot - pull) / math.sqrt(width)).astype(bf16)
        qkv_cot_ref[f, :, :width] = dot(scores_cot, keys, NN).astype(bf16)
        qkv_cot_ref[f, :, width : 2 * width] = dot(scores_cot, queries, TN).astype(bf16)
        qkv_cot_ref[f, :, 2 * width :] = dot(prob.astype(bf16), cot, TN).astype(bf16)
    grad_ref[...] = dot(
        qkv_cot_ref[...].reshape(rows, 3 * width), normed_ref[...].reshape(rows, width), TN
    )
    columns = grad_ref.shape[0] // (2 * PIECES)
    short = keep_ref.shape[1] - columns
    left = lax.broadcasted_iota(jnp.int32, (short, LANES), 1) < LANES // 2
    first = core_ref[0] == 0
    for group in range(groups):
        for chip in range(PIECES):
            pair = []
            for core in range(2):
                top = (2 * chip + core) * columns
                low = top + columns - short
                upper = grad_ref[top : top + short, LANES : 2 * LANES]
                lower = grad_ref[low : low + short, LANES : 2 * LANES]
                if group == 0:
                    lower = pltpu.roll(lower, LANES // 2, 1)
                else:
                    upper = pltpu.roll(upper, LANES // 2, 1)
                side = 2 * group * LANES
                pair.append(
                    jnp.concatenate(
                        [
                            grad_ref[top : top + columns, side : side + LANES],
                            jnp.where(left, upper, lower),
                        ],
                        axis=0,
                    )
                )
            keep_ref[group * PIECES + chip] = jnp.where(first, pair[0], pair[1]).astype(bf16)
            send_ref[group * PIECES + chip] = jnp.where(first, pair[1], pair[0]).astype(bf16)


def turn_kernel(got_ref, turn_ref, out_ref):
    columns, short = 72, got_ref.shape[1] - 72
    total = got_ref[0].astype(f32)
    for i in range(1, got_ref.shape[0]):
        total = total + got_ref[i].astype(f32)
    narrow = total[columns:]
    other = pltpu.roll(narrow, LANES // 2, 1)
    narrow = jnp.concatenate([narrow, other[2 * short - columns :]], axis=0)
    turned = dot(turn_ref[0], total[:columns].astype(bf16), NT)
    turned = turned + dot(turn_ref[1], narrow.astype(bf16), NT)
    turned = turned.astype(bf16).reshape(out_ref.shape[0], 16, columns)
    out_ref[...] = jnp.zeros_like(out_ref)
    out_ref[:, :, :columns] = turned


def input_kernel(clip_ref, gain_ref, weight_ref, qkv_cot_ref, upstream_ref, out_ref):
    frames, positions, width = clip_ref.shape
    for f in range(frames):
        features = clip_ref[f].astype(f32)
        squares = jnp.mean(features * features, axis=-1, keepdims=True)
        scale = lax.rsqrt(squares + 1e-06)
        cot = dot(qkv_cot_ref[f], weight_ref[...], NT) * gain_ref[...]
        along = jnp.mean(features * cot, axis=-1, keepdims=True)
        direct = scale * cot - features * (scale * scale * scale * along)
        out_ref[f] = (upstream_ref[f].astype(f32) + direct).astype(bf16)


def whole(count):
    return [pl.BlockSpec(memory_space=pltpu.VMEM)] * count


def call(kernel, outs, args, flops, limit, scratch=(), specs=None):
    moved = sum(a.size * a.dtype.itemsize for a in args)
    moved += sum(math.prod(s) * jnp.dtype(d).itemsize for s, d in outs)
    return pl.pallas_call(
        kernel,
        out_shape=tuple(jax.ShapeDtypeStruct(s, d) for s, d in outs),
        in_specs=specs or whole(len(args)),
        out_specs=tuple(whole(len(outs))),
        scratch_shapes=list(scratch),
        cost_estimate=pl.CostEstimate(flops=flops, bytes_accessed=moved, transcendentals=0),
        compiler_params=pltpu.CompilerParams(vmem_limit_bytes=limit << 20),
    )(*args)


def spread(block, axes):
    count = math.prod(lax.axis_size(a) for a in axes)
    return lax.all_to_all(
        jnp.broadcast_to(block[None], (count,) + block.shape), axes, 0, 0, tiled=True
    )


def tap_column(shard):
    taps, held, wide = shard.shape
    lanes, parts = wide // LANES, held // 4
    tiles = shard.reshape(taps, 2, parts, 2, lanes, LANES).transpose(1, 0, 4, 2, 3, 5)
    count = taps * lanes * parts
    tiles = tiles.reshape(2, count, 2, LANES)
    tiles = jnp.concatenate([tiles, jnp.zeros((2, PIECES * TILES - count, 2, LANES), bf16)], 1)
    tiles = tiles.reshape(2 * PIECES, TILES, 2, LANES)
    place = lax.axis_index("y") * lax.axis_size("xl") + lax.axis_index("xl")
    place = place + lax.axis_index("co") * PIECES
    column = spread(lax.dynamic_index_in_dim(tiles, place, 0, keepdims=False), ("z",))
    return column.transpose(1, 0, 2, 3).reshape(TILES, -1, LANES)


def channel_order(width):
    depth, groups = lax.axis_size("z"), lax.axis_size("xh")
    held = width // (depth * groups)
    parts = held // 4
    place = jnp.arange(width)
    row, place = place % 2, place // 2
    level, place = place % depth, place // depth
    part, place = place % parts, place // parts
    group, half = place % groups, place // groups
    side = jnp.where(lax.axis_index("co") == 0, half, 1 - half)
    channel = held * (group * depth + level) + (held // 2) * side + 2 * part + row
    return (channel[:, None] == jnp.arange(width)[None, :]).astype(bf16)


def turn_orders(held, depth):
    group = lax.axis_index("xh")
    row = jnp.arange(depth * 16)
    channel = jnp.where(row % 16 < held, row // 16 * held + row % 16, -1)[:, None]
    lane = jnp.arange(LANES)[None, :]
    wide = channel == lane + 64 * group
    narrow = (channel == lane + LANES * (1 - group)) & (lane < 64)
    return jnp.stack([wide, narrow]).astype(bf16)


def on_device(clip_input, norm_gain, qkv_weight, out_weight, time_weight, upsample_cotangent):
    clip = clip_input[0]
    cotangent = upsample_cotangent[0]
    frames, positions, width = clip.shape
    wide = cotangent.shape[-1]
    rows = frames * positions
    slabs = math.prod(lax.axis_size(a) for a in TM)
    clips = math.prod(lax.axis_size(a) for a in DP)
    gain = norm_gain[None]

    incoming = lax.ppermute(cotangent, TM, [(i + 1, i) for i in range(slabs - 1)])
    column = tap_column(time_weight)
    normed, qkv, prob = call(
        forward_kernel,
        [((frames, positions, width), bf16), ((frames, positions, 3 * width), bf16),
         ((frames, positions, positions), f32)],
        [clip, gain, qkv_weight],
        2 * rows * width * (3 * width + positions),
        16,
    )
    depth = lax.axis_size("z")
    held = width // clips
    order = channel_order(width)
    turn = turn_orders(held, depth)
    core = lax.axis_index("co").reshape(1)
    column, incoming, normed, qkv, prob, order, turn = lax.optimization_barrier(
        (column, incoming, normed, qkv, prob, order, turn)
    )
    own = spread(column, PLANE)
    swap = [(0, 1), (1, 0)]
    other = lax.ppermute(own, "co", swap)

    chips = own.shape[0]
    packed = ((chips, 112, LANES), bf16)
    upstream, qkv_cot, keep, send = call(
        backward_kernel,
        [((frames, positions, width), bf16), ((frames, positions, 3 * width), bf16), packed, packed],
        [core, cotangent, incoming, own, other, order, out_weight, qkv, prob, normed],
        2 * rows * width * (3 * wide + 2 * width + 4 * positions + 3 * width),
        32,
        [pltpu.VMEM((3, width, wide), bf16), pltpu.VMEM(cotangent.shape, bf16),
         pltpu.VMEM(cotangent.shape, bf16), pltpu.VMEM((3 * width, width), f32),
         pltpu.SemaphoreType.DMA((2,))],
        [pl.BlockSpec(memory_space=pltpu.SMEM)] + [pl.BlockSpec(memory_space=pl.ANY)] * 2 + whole(7),
    )
    share = keep.astype(f32) + lax.ppermute(send, "co", swap).astype(f32)
    share = lax.all_to_all(share.astype(bf16), PLANE, 0, 0, tiled=True)
    (input_grad,) = call(
        input_kernel,
        [((frames, positions, width), bf16)],
        [clip, gain, qkv_weight, qkv_cot, upstream],
        2 * rows * width * 3 * width,
        16,
    )
    (share,) = call(
        turn_kernel,
        [((depth, 16, LANES), bf16)],
        [share, turn],
        2 * depth * 16 * 72 * 2 * LANES,
        16,
    )
    share = lax.all_to_all(share, "z", 0, 0, tiled=True)
    qkv_grad = jnp.sum(share[:, :held, : 3 * width // slabs].astype(f32), axis=0)
    return (input_grad[None], qkv_grad)


def solution(mesh):
    split = Mesh(mesh.devices.reshape(SIZES), AXES)
    in_specs = (
        P(DP, TM, None, None),
        P(),
        P(),
        P(),
        P(None, DP, None),
        P(DP, TM, None, None),
    )
    out_specs = (P(DP, TM, None, None), P(DP, TM))
    return jax.shard_map(
        on_device, mesh=split, in_specs=in_specs, out_specs=out_specs, check_vma=False
    )
```

```python
import math

import jax
import jax.numpy as jnp
from jax import lax
from jax.experimental import pallas as pl
from jax.experimental.pallas import tpu as pltpu
from jax.sharding import Mesh
from jax.sharding import PartitionSpec as P

AXES = ("xh", "z", "y", "xl", "co")
SIZES = (2, 16, 4, 2, 2)
DP = ("xh", "z")
TM = ("y", "xl", "co")
PLANE = ("xh", "y", "xl")
PIECES = 8
TILES = 7
LANES = 128
bf16, f32 = jnp.bfloat16, jnp.float32


def dot(a, b, contract):
    return lax.dot_general(a, b, (contract, ((), ())), preferred_element_type=f32)


NN, NT, TN = ((1,), (0,)), ((1,), (1,)), ((0,), (0,))


def forward_kernel(clip_ref, gain_ref, weight_ref, normed_ref, qkv_ref, prob_ref):
    frames, _, width = clip_ref.shape
    for f in range(frames):
        features = clip_ref[f].astype(f32)
        squares = jnp.mean(features * features, axis=-1, keepdims=True)
        normed = (features * lax.rsqrt(squares + 1e-06) * gain_ref[...]).astype(bf16)
        normed_ref[f] = normed
        qkv = dot(normed, weight_ref[...], NN).astype(bf16)
        qkv_ref[f] = qkv
        scores = dot(qkv[:, :width], qkv[:, width : 2 * width], NT) / math.sqrt(width)
        raised = jnp.exp(scores - jnp.max(scores, axis=-1, keepdims=True))
        prob_ref[f] = raised / jnp.sum(raised, axis=-1, keepdims=True)


def backward_kernel(
    core_ref, cot_any, next_any, own_ref, other_ref, order_ref, out_weight_ref, qkv_ref, prob_ref,
    normed_ref, upstream_ref, qkv_cot_ref, keep_ref, send_ref, taps_ref, cot_ref, next_ref,
    grad_ref, sems,
):
    frames, positions, width = upstream_ref.shape
    rows = frames * positions
    wide = cot_ref.shape[-1]
    taps = taps_ref.shape[0]
    block = own_ref.shape[2]
    groups = own_ref.shape[0] // PIECES
    lanes = wide // LANES
    parts = width // (2 * groups * block)
    copies = [
        pltpu.make_async_copy(cot_any, cot_ref, sems.at[0]),
        pltpu.make_async_copy(next_any, next_ref, sems.at[1]),
    ]
    for copy in copies:
        copy.start()
    for half, source in enumerate((own_ref, other_ref)):
        for group in range(groups):
            for tile in range(taps * lanes * parts):
                tap, rest = divmod(tile, lanes * parts)
                lane, part = divmod(rest, parts)
                start = ((half * groups + group) * parts + part) * block
                taps_ref[tap, start : start + block, lane * LANES : (lane + 1) * LANES] = source[
                    group * PIECES + tile // TILES, tile % TILES
                ]
    for copy in copies:
        copy.wait()
    middle = jnp.concatenate([cot_ref[1], next_ref[0]], axis=0)
    total = dot(cot_ref[...].reshape(rows, wide), taps_ref[2], NT)
    total = total + dot(middle, taps_ref[1], NT)
    total = total + dot(next_ref[...].reshape(rows, wide), taps_ref[0], NT)
    upstream = dot(total.astype(bf16), order_ref[...], NN).astype(bf16)
    upstream_ref[...] = upstream.reshape(upstream_ref.shape)
    mixed_cot = dot(upstream, out_weight_ref[...], NT).astype(bf16)
    for f in range(frames):
        cot = mixed_cot[f * positions : (f + 1) * positions]
        prob = prob_ref[f]
        queries = qkv_ref[f, :, :width]
        keys = qkv_ref[f, :, width : 2 * width]
        values = qkv_ref[f, :, 2 * width :]
        weights_cot = dot(cot, values, NT).astype(bf16).astype(f32)
        pull = jnp.sum(weights_cot * prob, axis=-1, keepdims=True)
        scores_cot = (prob * (weights_cot - pull) / math.sqrt(width)).astype(bf16)
        qkv_cot_ref[f, :, :width] = dot(scores_cot, keys, NN).astype(bf16)
        qkv_cot_ref[f, :, width : 2 * width] = dot(scores_cot, queries, TN).astype(bf16)
        qkv_cot_ref[f, :, 2 * width :] = dot(prob.astype(bf16), cot, TN).astype(bf16)
    grad_ref[...] = dot(
        qkv_cot_ref[...].reshape(rows, 3 * width), normed_ref[...].reshape(rows, width), TN
    )
    columns = grad_ref.shape[0] // (2 * PIECES)
    short = keep_ref.shape[1] - columns
    left = lax.broadcasted_iota(jnp.int32, (short, LANES), 1) < LANES // 2
    first = core_ref[0] == 0
    for group in range(groups):
        for chip in range(PIECES):
            pair = []
            for core in range(2):
                top = (2 * chip + core) * columns
                low = top + columns - short
                upper = grad_ref[top : top + short, LANES : 2 * LANES]
                lower = grad_ref[low : low + short, LANES : 2 * LANES]
                if group == 0:
                    lower = pltpu.roll(lower, LANES // 2, 1)
                else:
                    upper = pltpu.roll(upper, LANES // 2, 1)
                side = 2 * group * LANES
                pair.append(
                    jnp.concatenate(
                        [
                            grad_ref[top : top + columns, side : side + LANES],
                            jnp.where(left, upper, lower),
                        ],
                        axis=0,
                    )
                )
            keep_ref[group * PIECES + chip] = jnp.where(first, pair[0], pair[1]).astype(bf16)
            send_ref[group * PIECES + chip] = jnp.where(first, pair[1], pair[0]).astype(bf16)


def turn_kernel(got_ref, turn_ref, out_ref):
    columns, short = 72, got_ref.shape[1] - 72
    total = got_ref[0].astype(f32)
    for i in range(1, got_ref.shape[0]):
        total = total + got_ref[i].astype(f32)
    narrow = total[columns:]
    other = pltpu.roll(narrow, LANES // 2, 1)
    narrow = jnp.concatenate([narrow, other[2 * short - columns :]], axis=0)
    turned = dot(turn_ref[0], total[:columns].astype(bf16), NT)
    turned = turned + dot(turn_ref[1], narrow.astype(bf16), NT)
    turned = turned.astype(bf16).reshape(out_ref.shape[0], 16, columns)
    out_ref[...] = jnp.zeros_like(out_ref)
    out_ref[:, :, :columns] = turned


def input_kernel(clip_ref, gain_ref, weight_ref, qkv_cot_ref, upstream_ref, out_ref):
    frames, _, _ = clip_ref.shape
    for f in range(frames):
        features = clip_ref[f].astype(f32)
        squares = jnp.mean(features * features, axis=-1, keepdims=True)
        scale = lax.rsqrt(squares + 1e-06)
        cot = dot(qkv_cot_ref[f], weight_ref[...], NT) * gain_ref[...]
        along = jnp.mean(features * cot, axis=-1, keepdims=True)
        direct = scale * cot - features * (scale * scale * scale * along)
        out_ref[f] = (upstream_ref[f].astype(f32) + direct).astype(bf16)


def whole(count):
    return [pl.BlockSpec(memory_space=pltpu.VMEM)] * count


def call(kernel, outs, args, flops, limit, scratch=(), specs=None):
    moved = sum(a.size * a.dtype.itemsize for a in args)
    moved += sum(math.prod(s) * jnp.dtype(d).itemsize for s, d in outs)
    return pl.pallas_call(
        kernel,
        out_shape=tuple(jax.ShapeDtypeStruct(s, d) for s, d in outs),
        in_specs=specs or whole(len(args)),
        out_specs=tuple(whole(len(outs))),
        scratch_shapes=list(scratch),
        cost_estimate=pl.CostEstimate(flops=flops, bytes_accessed=moved, transcendentals=0),
        compiler_params=pltpu.CompilerParams(vmem_limit_bytes=limit << 20),
    )(*args)


def spread(block, axes):
    count = math.prod(lax.axis_size(a) for a in axes)
    return lax.all_to_all(
        jnp.broadcast_to(block[None], (count,) + block.shape), axes, 0, 0, tiled=True
    )


def tap_column(shard, core, group):
    taps, held, wide = shard.shape
    lanes, parts = wide // LANES, held // 4
    tiles = shard.reshape(taps, 2, parts, 2, lanes, LANES).transpose(1, 0, 4, 2, 3, 5)
    count = taps * lanes * parts
    tiles = tiles.reshape(2, count, 2, LANES)
    tiles = jnp.concatenate([tiles, jnp.zeros((2, PIECES * TILES - count, 2, LANES), bf16)], 1)
    tiles = tiles.reshape(2 * PIECES, TILES, 2, LANES)
    place = lax.axis_index("y") * lax.axis_size("xl") + lax.axis_index("xl")
    place = place + core * PIECES
    piece = lax.dynamic_index_in_dim(tiles, place, 0, keepdims=False)
    piece, core, group = lax.optimization_barrier((piece, core, group))
    column = spread(piece, ("z",))
    return column.transpose(1, 0, 2, 3).reshape(TILES, -1, LANES), core, group


def channel_order(width, core):
    depth, groups = lax.axis_size("z"), lax.axis_size("xh")
    held = width // (depth * groups)
    parts = held // 4
    place = jnp.arange(width)
    row, place = place % 2, place // 2
    level, place = place % depth, place // depth
    part, place = place % parts, place // parts
    group, half = place % groups, place // groups
    side = jnp.where(core == 0, half, 1 - half)
    channel = held * (group * depth + level) + (held // 2) * side + 2 * part + row
    return (channel[:, None] == jnp.arange(width)[None, :]).astype(bf16)


def turn_orders(held, depth, group):
    row = jnp.arange(depth * 16)
    channel = jnp.where(row % 16 < held, row // 16 * held + row % 16, -1)[:, None]
    lane = jnp.arange(LANES)[None, :]
    wide = channel == lane + 64 * group
    narrow = (channel == lane + LANES * (1 - group)) & (lane < 64)
    return jnp.stack([wide, narrow]).astype(bf16)


def on_device(clip_input, norm_gain, qkv_weight, out_weight, time_weight, upsample_cotangent):
    clip = clip_input[0]
    cotangent = upsample_cotangent[0]
    frames, positions, width = clip.shape
    wide = cotangent.shape[-1]
    rows = frames * positions
    slabs = math.prod(lax.axis_size(a) for a in TM)
    clips = math.prod(lax.axis_size(a) for a in DP)
    gain = norm_gain[None]

    depth = lax.axis_size("z")
    held = width // clips
    swap = [(0, 1), (1, 0)]
    incoming = lax.ppermute(cotangent, TM, [(i + 1, i) for i in range(slabs - 1)])
    column, core, group = tap_column(
        time_weight, lax.axis_index("co"), lax.axis_index("xh")
    )
    column, core, group = lax.optimization_barrier((column, core, group))
    own = spread(column, PLANE)
    own, clip, core, group = lax.optimization_barrier((own, clip, core, group))
    other = lax.ppermute(own, "co", swap)
    normed, qkv, prob = call(
        forward_kernel,
        [((frames, positions, width), bf16), ((frames, positions, 3 * width), bf16),
         ((frames, positions, positions), f32)],
        [clip, gain, qkv_weight],
        2 * rows * width * (3 * width + positions),
        16,
    )
    order = channel_order(width, core)
    turn = turn_orders(held, depth, group)
    core = core.reshape(1)

    chips = own.shape[0]
    packed = ((chips, 112, LANES), bf16)
    upstream, qkv_cot, keep, send = call(
        backward_kernel,
        [((frames, positions, width), bf16), ((frames, positions, 3 * width), bf16), packed, packed],
        [core, cotangent, incoming, own, other, order, out_weight, qkv, prob, normed],
        2 * rows * width * (3 * wide + 2 * width + 4 * positions + 3 * width),
        32,
        [pltpu.VMEM((3, width, wide), bf16), pltpu.VMEM(cotangent.shape, bf16),
         pltpu.VMEM(cotangent.shape, bf16), pltpu.VMEM((3 * width, width), f32),
         pltpu.SemaphoreType.DMA((2,))],
        [pl.BlockSpec(memory_space=pltpu.SMEM)] + [pl.BlockSpec(memory_space=pl.ANY)] * 2 + whole(7),
    )
    got = lax.ppermute(send, "co", swap)
    (input_grad,) = call(
        input_kernel,
        [((frames, positions, width), bf16)],
        [clip, gain, qkv_weight, qkv_cot, upstream],
        2 * rows * width * 3 * width,
        16,
    )
    got, input_grad, turn = lax.optimization_barrier((got, input_grad, turn))
    share = (keep.astype(f32) + got.astype(f32)).astype(bf16)
    share = lax.all_to_all(share, PLANE, 0, 0, tiled=True)
    (share,) = call(
        turn_kernel,
        [((depth, 16, LANES), bf16)],
        [share, turn],
        2 * depth * 16 * 72 * 2 * LANES,
        16,
    )
    share = lax.all_to_all(share, "z", 0, 0, tiled=True)
    qkv_grad = jnp.sum(share[:, :held, : 3 * width // slabs].astype(f32), axis=0)
    return (input_grad[None], qkv_grad)


def solution(mesh):
    split = Mesh(mesh.devices.reshape(SIZES), AXES)
    in_specs = (
        P(DP, TM, None, None),
        P(),
        P(),
        P(),
        P(None, DP, None),
        P(DP, TM, None, None),
    )
    out_specs = (P(DP, TM, None, None), P(DP, TM))

    return jax.shard_map(
        on_device, mesh=split, in_specs=in_specs, out_specs=out_specs, check_vma=False
    )
```

```python
import math

import jax
import jax.numpy as jnp
from jax import lax
from jax.experimental import pallas as pl
from jax.experimental.pallas import tpu as pltpu
from jax.sharding import Mesh
from jax.sharding import PartitionSpec as P

AXES = ("xh", "z", "y", "xl", "co")
SIZES = (2, 16, 4, 2, 2)
DP = ("xh", "z")
TM = ("y", "xl", "co")
PLANE = ("xh", "y", "xl")
PIECES = 8
TILES = 7
LANES = 128
bf16, f32 = jnp.bfloat16, jnp.float32


def dot(a, b, contract):
    return lax.dot_general(a, b, (contract, ((), ())), preferred_element_type=f32)


NN, NT, TN = ((1,), (0,)), ((1,), (1,)), ((0,), (0,))


def forward_kernel(clip_ref, gain_ref, weight_ref, normed_ref, qkv_ref, prob_ref):
    frames, _, width = clip_ref.shape
    for f in range(frames):
        features = clip_ref[f].astype(f32)
        squares = jnp.mean(features * features, axis=-1, keepdims=True)
        normed = (features * lax.rsqrt(squares + 1e-06) * gain_ref[...]).astype(bf16)
        normed_ref[f] = normed
        qkv = dot(normed, weight_ref[...], NN).astype(bf16)
        qkv_ref[f] = qkv
        scores = dot(qkv[:, :width], qkv[:, width : 2 * width], NT) / math.sqrt(width)
        raised = jnp.exp(scores - jnp.max(scores, axis=-1, keepdims=True))
        prob_ref[f] = raised / jnp.sum(raised, axis=-1, keepdims=True)


def backward_kernel(
    core_ref, cot_ref, next_any, own_ref, other_ref, order_ref, out_weight_ref, qkv_ref, prob_ref,
    normed_ref, upstream_ref, qkv_cot_ref, keep_ref, send_ref, taps_ref, next_ref, grad_ref, sem,
):
    frames, positions, width = upstream_ref.shape
    rows = frames * positions
    wide = cot_ref.shape[-1]
    taps = taps_ref.shape[0]
    block = own_ref.shape[2]
    groups = own_ref.shape[0] // PIECES
    lanes = wide // LANES
    parts = width // (2 * groups * block)
    copy = pltpu.make_async_copy(next_any, next_ref, sem)
    copy.start()
    for half, source in enumerate((own_ref, other_ref)):
        for group in range(groups):
            for tile in range(taps * lanes * parts):
                tap, rest = divmod(tile, lanes * parts)
                lane, part = divmod(rest, parts)
                start = ((half * groups + group) * parts + part) * block
                taps_ref[tap, start : start + block, lane * LANES : (lane + 1) * LANES] = source[
                    group * PIECES + tile // TILES, tile % TILES
                ]
    total = dot(cot_ref[...].reshape(rows, wide), taps_ref[2], NT)
    copy.wait()
    middle = jnp.concatenate([cot_ref[1], next_ref[0]], axis=0)
    total = total + dot(middle, taps_ref[1], NT)
    total = total + dot(next_ref[...].reshape(rows, wide), taps_ref[0], NT)
    upstream = dot(total.astype(bf16), order_ref[...], NN).astype(bf16)
    upstream_ref[...] = upstream.reshape(upstream_ref.shape)
    mixed_cot = dot(upstream, out_weight_ref[...], NT).astype(bf16)
    for f in range(frames):
        cot = mixed_cot[f * positions : (f + 1) * positions]
        prob = prob_ref[f]
        queries = qkv_ref[f, :, :width]
        keys = qkv_ref[f, :, width : 2 * width]
        values = qkv_ref[f, :, 2 * width :]
        weights_cot = dot(cot, values, NT).astype(bf16).astype(f32)
        pull = jnp.sum(weights_cot * prob, axis=-1, keepdims=True)
        scores_cot = (prob * (weights_cot - pull) / math.sqrt(width)).astype(bf16)
        qkv_cot_ref[f, :, :width] = dot(scores_cot, keys, NN).astype(bf16)
        qkv_cot_ref[f, :, width : 2 * width] = dot(scores_cot, queries, TN).astype(bf16)
        qkv_cot_ref[f, :, 2 * width :] = dot(prob.astype(bf16), cot, TN).astype(bf16)
    grad_ref[...] = dot(
        qkv_cot_ref[...].reshape(rows, 3 * width), normed_ref[...].reshape(rows, width), TN
    )
    columns = grad_ref.shape[0] // (2 * PIECES)
    short = keep_ref.shape[1] - columns
    left = lax.broadcasted_iota(jnp.int32, (short, LANES), 1) < LANES // 2
    first = core_ref[0] == 0
    for group in range(groups):
        for chip in range(PIECES):
            pair = []
            for core in range(2):
                top = (2 * chip + core) * columns
                low = top + columns - short
                upper = grad_ref[top : top + short, LANES : 2 * LANES]
                lower = grad_ref[low : low + short, LANES : 2 * LANES]
                if group == 0:
                    lower = pltpu.roll(lower, LANES // 2, 1)
                else:
                    upper = pltpu.roll(upper, LANES // 2, 1)
                side = 2 * group * LANES
                pair.append(
                    jnp.concatenate(
                        [
                            grad_ref[top : top + columns, side : side + LANES],
                            jnp.where(left, upper, lower),
                        ],
                        axis=0,
                    )
                )
            keep_ref[group * PIECES + chip] = jnp.where(first, pair[0], pair[1]).astype(bf16)
            send_ref[group * PIECES + chip] = jnp.where(first, pair[1], pair[0]).astype(bf16)


def turn_kernel(got_ref, turn_ref, out_ref):
    columns, short = 72, got_ref.shape[1] - 72
    depth = out_ref.shape[0]
    total = got_ref[0].astype(f32)
    for i in range(1, got_ref.shape[0]):
        total = total + got_ref[i].astype(f32)
    narrow = total[columns:]
    other = pltpu.roll(narrow, LANES // 2, 1)
    empty = jnp.zeros((LANES - columns, LANES), f32)
    narrow = jnp.concatenate([narrow, other[2 * short - columns :], empty], axis=0)
    wide = jnp.concatenate([total[:columns], empty], axis=0)
    turned = dot(turn_ref[0], wide.astype(bf16), NT) + dot(turn_ref[1], narrow.astype(bf16), NT)
    first, last = turned[: depth * 8], turned[depth * 8 :]
    row = lax.broadcasted_iota(jnp.int32, first.shape, 0)
    lane = lax.broadcasted_iota(jnp.int32, first.shape, 1)
    last = jnp.where(
        lax.rem(row, 2) == 0, pltpu.roll(last, columns, 1), pltpu.roll(last, columns // 2, 1)
    )
    turned = jnp.where(lane < columns, first, last)
    out_ref[...] = turned.astype(bf16).reshape(out_ref.shape)


def final_kernel(got_ref, out_ref):
    columns = out_ref.shape[1]
    total = got_ref[0].astype(f32)
    for i in range(1, got_ref.shape[0]):
        total = total + got_ref[i].astype(f32)
    out_ref[0:8] = total[:, :columns]
    even = pltpu.roll(total, LANES - columns, 1)
    odd = pltpu.roll(total, LANES - columns // 2, 1)
    left = lax.broadcasted_iota(jnp.int32, (1, LANES), 1) < columns // 2
    for i in range(4):
        line = jnp.where(left, even[2 * i : 2 * i + 1], odd[2 * i + 1 : 2 * i + 2])
        out_ref[8 + i : 9 + i] = line[:, :columns]


def input_kernel(clip_ref, gain_ref, weight_ref, qkv_cot_ref, upstream_ref, out_ref):
    frames, _, _ = clip_ref.shape
    for f in range(frames):
        features = clip_ref[f].astype(f32)
        squares = jnp.mean(features * features, axis=-1, keepdims=True)
        scale = lax.rsqrt(squares + 1e-06)
        cot = dot(qkv_cot_ref[f], weight_ref[...], NT) * gain_ref[...]
        along = jnp.mean(features * cot, axis=-1, keepdims=True)
        direct = scale * cot - features * (scale * scale * scale * along)
        out_ref[f] = (upstream_ref[f].astype(f32) + direct).astype(bf16)


def whole(count):
    return [pl.BlockSpec(memory_space=pltpu.VMEM)] * count


def call(kernel, outs, args, flops, limit, scratch=(), specs=None):
    moved = sum(a.size * a.dtype.itemsize for a in args)
    moved += sum(math.prod(s) * jnp.dtype(d).itemsize for s, d in outs)
    return pl.pallas_call(
        kernel,
        out_shape=tuple(jax.ShapeDtypeStruct(s, d) for s, d in outs),
        in_specs=specs or whole(len(args)),
        out_specs=tuple(whole(len(outs))),
        scratch_shapes=list(scratch),
        cost_estimate=pl.CostEstimate(flops=flops, bytes_accessed=moved, transcendentals=0),
        compiler_params=pltpu.CompilerParams(vmem_limit_bytes=limit << 20),
    )(*args)


def spread(block, axes):
    count = math.prod(lax.axis_size(a) for a in axes)
    return lax.all_to_all(
        jnp.broadcast_to(block[None], (count,) + block.shape), axes, 0, 0, tiled=True
    )


def piece_kernel(place_ref, shard_ref, out_ref, tiles_ref):
    taps, held, wide = shard_ref.shape
    lanes, parts = wide // LANES, held // 4
    count = taps * lanes * parts
    slots = PIECES * TILES
    for side in range(2):
        for tile in range(count):
            tap, rest = divmod(tile, lanes * parts)
            lane, part = divmod(rest, parts)
            row = side * held // 2 + 2 * part
            tiles_ref[side * slots + tile] = shard_ref[
                tap, row : row + 2, lane * LANES : (lane + 1) * LANES
            ]
        for tile in range(count, slots):
            tiles_ref[side * slots + tile] = jnp.zeros((2, LANES), bf16)
    piece = tiles_ref[pl.ds(place_ref[0] * TILES, TILES)]
    for i in range(out_ref.shape[0]):
        out_ref[i] = piece


def tap_column(shard, core, group):
    place = lax.axis_index("y") * lax.axis_size("xl") + lax.axis_index("xl") + core * PIECES
    (piece,) = call(
        piece_kernel,
        [((lax.axis_size("z"), TILES, 2, LANES), bf16)],
        [place.reshape(1), shard],
        0,
        8,
        [pltpu.VMEM((2 * PIECES * TILES, 2, LANES), bf16)],
        [pl.BlockSpec(memory_space=pltpu.SMEM)] + whole(1),
    )
    piece, core, group = lax.optimization_barrier((piece, core, group))
    column = lax.all_to_all(piece, ("z",), 0, 0, tiled=True)
    return column.transpose(1, 0, 2, 3).reshape(TILES, -1, LANES), core, group


def channel_order(width, core):
    depth, groups = lax.axis_size("z"), lax.axis_size("xh")
    held = width // (depth * groups)
    parts = held // 4
    place = jnp.arange(width)
    row, place = place % 2, place // 2
    level, place = place % depth, place // depth
    part, place = place % parts, place // parts
    group, half = place % groups, place // groups
    side = jnp.where(core == 0, half, 1 - half)
    channel = held * (group * depth + level) + (held // 2) * side + 2 * part + row
    return (channel[:, None] == jnp.arange(width)[None, :]).astype(bf16)


def turn_orders(held, depth, group):
    row = jnp.arange(depth * 8)
    first = row // 8 * held + row % 8
    last = row // 8 * held + 8 + row % 8 // 2
    channel = jnp.concatenate([first, last])[:, None]
    lane = jnp.arange(LANES)[None, :]
    wide = channel == lane + 64 * group
    narrow = (channel == lane + LANES * (1 - group)) & (lane < 64)
    return jnp.stack([wide, narrow]).astype(bf16)


def on_device(clip_input, norm_gain, qkv_weight, out_weight, time_weight, upsample_cotangent):
    clip = clip_input[0]
    cotangent = upsample_cotangent[0]
    frames, positions, width = clip.shape
    wide = cotangent.shape[-1]
    rows = frames * positions
    slabs = math.prod(lax.axis_size(a) for a in TM)
    clips = math.prod(lax.axis_size(a) for a in DP)
    gain = norm_gain[None]

    depth = lax.axis_size("z")
    held = width // clips
    swap = [(0, 1), (1, 0)]
    incoming = lax.ppermute(cotangent, TM, [(i + 1, i) for i in range(slabs - 1)])
    column, core, group = tap_column(
        time_weight, lax.axis_index("co"), lax.axis_index("xh")
    )
    column, core, group = lax.optimization_barrier((column, core, group))
    own = spread(column, PLANE)
    own, clip, core, group = lax.optimization_barrier((own, clip, core, group))
    other = lax.ppermute(own, "co", swap)
    normed, qkv, prob = call(
        forward_kernel,
        [((frames, positions, width), bf16), ((frames, positions, 3 * width), bf16),
         ((frames, positions, positions), f32)],
        [clip, gain, qkv_weight],
        2 * rows * width * (3 * width + positions),
        16,
    )
    order = channel_order(width, core)
    turn = turn_orders(held, depth, group)
    core = core.reshape(1)

    chips = own.shape[0]
    packed = ((chips, 112, LANES), bf16)
    upstream, qkv_cot, keep, send = call(
        backward_kernel,
        [((frames, positions, width), bf16), ((frames, positions, 3 * width), bf16), packed, packed],
        [core, cotangent, incoming, own, other, order, out_weight, qkv, prob, normed],
        2 * rows * width * (3 * wide + 2 * width + 4 * positions + 3 * width),
        32,
        [pltpu.VMEM((3, width, wide), bf16), pltpu.VMEM(cotangent.shape, bf16),
         pltpu.VMEM((3 * width, width), f32), pltpu.SemaphoreType.DMA],
        [pl.BlockSpec(memory_space=pltpu.SMEM)] + whole(1) + [pl.BlockSpec(memory_space=pl.ANY)]
        + whole(7),
    )
    got = lax.ppermute(send, "co", swap)
    (input_grad,) = call(
        input_kernel,
        [((frames, positions, width), bf16)],
        [clip, gain, qkv_weight, qkv_cot, upstream],
        2 * rows * width * 3 * width,
        16,
    )
    got, input_grad, turn = lax.optimization_barrier((got, input_grad, turn))
    share = (keep.astype(f32) + got.astype(f32)).astype(bf16)
    share = lax.all_to_all(share, PLANE, 0, 0, tiled=True)
    (share,) = call(
        turn_kernel,
        [((depth, 8, LANES), bf16)],
        [share, turn],
        2 * depth * 16 * 72 * 2 * LANES,
        16,
    )
    share = lax.all_to_all(share, "z", 0, 0, tiled=True)
    (qkv_grad,) = call(final_kernel, [((held, 3 * width // slabs), f32)], [share], 0, 8)
    return (input_grad[None], qkv_grad)


def solution(mesh):
    split = Mesh(mesh.devices.reshape(SIZES), AXES)
    in_specs = (
        P(DP, TM, None, None),
        P(),
        P(),
        P(),
        P(None, DP, None),
        P(DP, TM, None, None),
    )
    out_specs = (P(DP, TM, None, None), P(DP, TM))

    return jax.shard_map(
        on_device, mesh=split, in_specs=in_specs, out_specs=out_specs, check_vma=False
    )
```

```python
import math

import jax
import jax.numpy as jnp
from jax import lax
from jax.experimental import pallas as pl
from jax.experimental.pallas import tpu as pltpu
from jax.sharding import Mesh
from jax.sharding import PartitionSpec as P

AXES = ("xh", "z", "y", "xl", "co")
SIZES = (2, 16, 4, 2, 2)
DP = ("xh", "z")
TM = ("y", "xl", "co")
PLANE = ("xh", "y", "xl")
PIECES = 8
TILES = 7
LANES = 128
bf16, f32 = jnp.bfloat16, jnp.float32


def dot(a, b, contract):
    return lax.dot_general(a, b, (contract, ((), ())), preferred_element_type=f32)


NN, NT, TN = ((1,), (0,)), ((1,), (1,)), ((0,), (0,))


def forward_kernel(
    clip_ref, gain_ref, weight_ref, order_ref, out_weight_ref,
    normed_ref, qkv_ref, prob_ref, out_order_ref,
):
    frames, _, width = clip_ref.shape
    out_order_ref[...] = dot(out_weight_ref[...], order_ref[...], NT).astype(bf16)
    for f in range(frames):
        features = clip_ref[f].astype(f32)
        squares = jnp.mean(features * features, axis=-1, keepdims=True)
        normed = (features * lax.rsqrt(squares + 1e-06) * gain_ref[...]).astype(bf16)
        normed_ref[f] = normed
        qkv = dot(normed, weight_ref[...], NN).astype(bf16)
        qkv_ref[f] = qkv
        scores = dot(qkv[:, :width], qkv[:, width : 2 * width], NT) / math.sqrt(width)
        raised = jnp.exp(scores - jnp.max(scores, axis=-1, keepdims=True))
        prob_ref[f] = raised / jnp.sum(raised, axis=-1, keepdims=True)


def backward_kernel(
    core_ref, cot_ref, next_any, own_ref, other_ref, order_ref, out_weight_ref, qkv_ref, prob_ref,
    normed_ref, upstream_ref, qkv_cot_ref, keep_ref, send_ref, grad_ref, next_ref, sem,
):
    frames, positions, width = upstream_ref.shape
    rows = frames * positions
    wide = cot_ref.shape[-1]
    block = own_ref.shape[2]
    groups = own_ref.shape[0] // PIECES
    lanes = wide // LANES
    parts = width // (2 * groups * block)

    copy = pltpu.make_async_copy(next_any, next_ref, sem)
    copy.start()

    def taps_of(tap):
        columns = []
        for lane in range(lanes):
            column = []
            for source in (own_ref, other_ref):
                for group in range(groups):
                    for part in range(parts):
                        tile = (tap * lanes + lane) * parts + part
                        column.append(source[group * PIECES + tile // TILES, tile % TILES])
            columns.append(jnp.concatenate(column, axis=0))
        return columns

    total = dot(cot_ref[...].reshape(rows, wide), jnp.concatenate(taps_of(2), axis=1), NT)
    copy.wait()
    middle = jnp.concatenate([cot_ref[1], next_ref[0]], axis=0)
    seen = jnp.concatenate([middle, next_ref[...].reshape(rows, wide)], axis=1)
    total = total + dot(seen, jnp.concatenate(taps_of(1) + taps_of(0), axis=1), NT)
    arrived = total.astype(bf16)
    mixed_cot = dot(arrived, out_weight_ref[...], NT).astype(bf16)
    cots = [mixed_cot[f * positions : (f + 1) * positions] for f in range(frames)]
    weights_cots = [
        dot(cots[f], qkv_ref[f, :, 2 * width :], NT).astype(bf16).astype(f32)
        for f in range(frames)
    ]
    for f in range(frames):
        qkv_cot_ref[f, :, 2 * width :] = dot(prob_ref[f].astype(bf16), cots[f], TN).astype(bf16)
    scores_cots = []
    for f in range(frames):
        prob = prob_ref[f]
        pull = jnp.sum(weights_cots[f] * prob, axis=-1, keepdims=True)
        scores_cots.append((prob * (weights_cots[f] - pull) / math.sqrt(width)).astype(bf16))
    normed = normed_ref[...].reshape(rows, width)

    for f in range(frames):
        qkv_cot_ref[f, :, :width] = dot(
            scores_cots[f], qkv_ref[f, :, width : 2 * width], NN
        ).astype(bf16)
    for f in range(frames):
        qkv_cot_ref[f, :, width : 2 * width] = dot(
            scores_cots[f], qkv_ref[f, :, :width], TN
        ).astype(bf16)
    upstream_ref[...] = dot(arrived, order_ref[...], NN).astype(bf16).reshape(upstream_ref.shape)
    grad_ref[...] = dot(qkv_cot_ref[...].reshape(rows, 3 * width), normed, TN)
    columns = grad_ref.shape[0] // (2 * PIECES)
    short = keep_ref.shape[1] - columns
    left = lax.broadcasted_iota(jnp.int32, (short, LANES), 1) < LANES // 2
    for out_ref, core in ((keep_ref, core_ref[0]), (send_ref, 1 - core_ref[0])):
        for group in range(groups):
            for chip in range(PIECES):
                top = pl.multiple_of((2 * chip + core) * columns, 8)
                low = pl.multiple_of(top + columns - short, 8)
                upper = grad_ref[pl.ds(top, short), LANES : 2 * LANES]
                lower = grad_ref[pl.ds(low, short), LANES : 2 * LANES]
                if group == 0:
                    lower = pltpu.roll(lower, LANES // 2, 1)
                else:
                    upper = pltpu.roll(upper, LANES // 2, 1)
                side = 2 * group * LANES
                wide_part = grad_ref[pl.ds(top, columns), side : side + LANES]
                out_ref[group * PIECES + chip] = jnp.concatenate(
                    [wide_part, jnp.where(left, upper, lower)], axis=0
                ).astype(bf16)


def turn_kernel(got_ref, turn_ref, out_ref):
    columns, short = 72, got_ref.shape[1] - 72
    depth = out_ref.shape[0]
    total = got_ref[0].astype(f32)
    for i in range(1, got_ref.shape[0]):
        total = total + got_ref[i].astype(f32)
    narrow = total[columns:]
    other = pltpu.roll(narrow, LANES // 2, 1)
    empty = jnp.zeros((LANES - columns, LANES), f32)
    narrow = jnp.concatenate([narrow, other[2 * short - columns :], empty], axis=0)
    wide = jnp.concatenate([total[:columns], empty], axis=0)
    turned = dot(turn_ref[0], wide.astype(bf16), NT) + dot(turn_ref[1], narrow.astype(bf16), NT)
    first, last = turned[: depth * 8], turned[depth * 8 :]
    row = lax.broadcasted_iota(jnp.int32, first.shape, 0)
    lane = lax.broadcasted_iota(jnp.int32, first.shape, 1)
    last = jnp.where(
        lax.rem(row, 2) == 0, pltpu.roll(last, columns, 1), pltpu.roll(last, columns // 2, 1)
    )
    turned = jnp.where(lane < columns, first, last)
    out_ref[...] = turned.astype(bf16).reshape(out_ref.shape)


def final_kernel(got_ref, out_ref):
    columns = out_ref.shape[1]
    total = got_ref[0].astype(f32)
    for i in range(1, got_ref.shape[0]):
        total = total + got_ref[i].astype(f32)
    out_ref[0:8] = total[:, :columns]
    even = pltpu.roll(total, LANES - columns, 1)
    odd = pltpu.roll(total, LANES - columns // 2, 1)
    left = lax.broadcasted_iota(jnp.int32, (1, LANES), 1) < columns // 2
    for i in range(4):
        line = jnp.where(left, even[2 * i : 2 * i + 1], odd[2 * i + 1 : 2 * i + 2])
        out_ref[8 + i : 9 + i] = line[:, :columns]


def input_kernel(clip_ref, gain_ref, weight_ref, qkv_cot_ref, upstream_ref, out_ref):
    frames, _, _ = clip_ref.shape
    for f in range(frames):
        features = clip_ref[f].astype(f32)
        squares = jnp.mean(features * features, axis=-1, keepdims=True)
        scale = lax.rsqrt(squares + 1e-06)
        cot = dot(qkv_cot_ref[f], weight_ref[...], NT) * gain_ref[...]
        along = jnp.mean(features * cot, axis=-1, keepdims=True)
        direct = scale * cot - features * (scale * scale * scale * along)
        out_ref[f] = (upstream_ref[f].astype(f32) + direct).astype(bf16)


def whole(count):
    return [pl.BlockSpec(memory_space=pltpu.VMEM)] * count


def call(kernel, outs, args, flops, limit, scratch=(), specs=None):
    moved = sum(a.size * a.dtype.itemsize for a in args)
    moved += sum(math.prod(s) * jnp.dtype(d).itemsize for s, d in outs)
    return pl.pallas_call(
        kernel,
        out_shape=tuple(jax.ShapeDtypeStruct(s, d) for s, d in outs),
        in_specs=specs or whole(len(args)),
        out_specs=tuple(whole(len(outs))),
        scratch_shapes=list(scratch),
        cost_estimate=pl.CostEstimate(flops=flops, bytes_accessed=moved, transcendentals=0),
        compiler_params=pltpu.CompilerParams(vmem_limit_bytes=limit << 20),
    )(*args)


def spread(block, axes):
    count = math.prod(lax.axis_size(a) for a in axes)
    return lax.all_to_all(
        jnp.broadcast_to(block[None], (count,) + block.shape), axes, 0, 0, tiled=True
    )


def piece_kernel(place_ref, shard_ref, out_ref, tiles_ref):
    taps, held, wide = shard_ref.shape
    lanes, parts = wide // LANES, held // 4
    count = taps * lanes * parts
    slots = PIECES * TILES
    for side in range(2):
        for tile in range(count):
            tap, rest = divmod(tile, lanes * parts)
            lane, part = divmod(rest, parts)
            row = side * held // 2 + 2 * part
            tiles_ref[side * slots + tile] = shard_ref[
                tap, row : row + 2, lane * LANES : (lane + 1) * LANES
            ]
        for tile in range(count, slots):
            tiles_ref[side * slots + tile] = jnp.zeros((2, LANES), bf16)
    piece = tiles_ref[pl.ds(place_ref[0] * TILES, TILES)]
    for i in range(out_ref.shape[0]):
        out_ref[i] = piece


def tap_column(shard, core, group):
    place = lax.axis_index("y") * lax.axis_size("xl") + lax.axis_index("xl") + core * PIECES
    (piece,) = call(
        piece_kernel,
        [((lax.axis_size("z"), TILES, 2, LANES), bf16)],
        [place.reshape(1), shard],
        0,
        8,
        [pltpu.VMEM((2 * PIECES * TILES, 2, LANES), bf16)],
        [pl.BlockSpec(memory_space=pltpu.SMEM)] + whole(1),
    )
    piece, core, group = lax.optimization_barrier((piece, core, group))
    column = lax.all_to_all(piece, ("z",), 0, 0, tiled=True)
    return column.transpose(1, 0, 2, 3).reshape(TILES, -1, LANES), core, group


def channel_order(width, core):
    depth, groups = lax.axis_size("z"), lax.axis_size("xh")
    held = width // (depth * groups)
    parts = held // 4
    place = jnp.arange(width)
    row, place = place % 2, place // 2
    level, place = place % depth, place // depth
    part, place = place % parts, place // parts
    group, half = place % groups, place // groups
    side = jnp.where(core == 0, half, 1 - half)
    channel = held * (group * depth + level) + (held // 2) * side + 2 * part + row
    return (channel[:, None] == jnp.arange(width)[None, :]).astype(bf16)


def turn_orders(held, depth, group):
    row = jnp.arange(depth * 8)
    first = row // 8 * held + row % 8
    last = row // 8 * held + 8 + row % 8 // 2
    channel = jnp.concatenate([first, last])[:, None]
    lane = jnp.arange(LANES)[None, :]
    wide = channel == lane + 64 * group
    narrow = (channel == lane + LANES * (1 - group)) & (lane < 64)
    return jnp.stack([wide, narrow]).astype(bf16)


def on_device(clip_input, norm_gain, qkv_weight, out_weight, time_weight, upsample_cotangent):
    clip = clip_input[0]
    cotangent = upsample_cotangent[0]
    frames, positions, width = clip.shape
    wide = cotangent.shape[-1]
    rows = frames * positions
    slabs = math.prod(lax.axis_size(a) for a in TM)
    clips = math.prod(lax.axis_size(a) for a in DP)
    gain = norm_gain[None]

    depth = lax.axis_size("z")
    held = width // clips
    swap = [(0, 1), (1, 0)]
    incoming = lax.ppermute(cotangent, TM, [(i + 1, i) for i in range(slabs - 1)])
    column, core, group = tap_column(
        time_weight, lax.axis_index("co"), lax.axis_index("xh")
    )
    column, core, group = lax.optimization_barrier((column, core, group))
    own = spread(column, PLANE)
    own, clip, core, group = lax.optimization_barrier((own, clip, core, group))
    other = lax.ppermute(own, "co", swap)
    order = channel_order(width, core)
    normed, qkv, prob, out_order = call(
        forward_kernel,
        [((frames, positions, width), bf16), ((frames, positions, 3 * width), bf16),
         ((frames, positions, positions), f32), ((width, width), bf16)],
        [clip, gain, qkv_weight, order, out_weight],
        2 * rows * width * (3 * width + positions),
        16,
    )
    turn = turn_orders(held, depth, group)
    core = core.reshape(1)

    chips = own.shape[0]
    packed = ((chips, 112, LANES), bf16)
    upstream, qkv_cot, keep, send = call(
        backward_kernel,
        [((frames, positions, width), bf16), ((frames, positions, 3 * width), bf16), packed, packed],
        [core, cotangent, incoming, own, other, order, out_order, qkv, prob, normed],
        2 * rows * width * (3 * wide + 2 * width + 4 * positions + 3 * width),
        32,
        [pltpu.VMEM((3 * width, width), f32), pltpu.VMEM(cotangent.shape, bf16),
         pltpu.SemaphoreType.DMA],
        [pl.BlockSpec(memory_space=pltpu.SMEM)] + whole(1) + [pl.BlockSpec(memory_space=pl.ANY)]
        + whole(7),
    )
    got = lax.ppermute(send, "co", swap)
    (input_grad,) = call(
        input_kernel,
        [((frames, positions, width), bf16)],
        [clip, gain, qkv_weight, qkv_cot, upstream],
        2 * rows * width * 3 * width,
        16,
    )
    got, input_grad, turn = lax.optimization_barrier((got, input_grad, turn))
    share = (keep.astype(f32) + got.astype(f32)).astype(bf16)
    share = lax.all_to_all(share, PLANE, 0, 0, tiled=True)
    (share,) = call(
        turn_kernel,
        [((depth, 8, LANES), bf16)],
        [share, turn],
        2 * depth * 16 * 72 * 2 * LANES,
        16,
    )
    share = lax.all_to_all(share, "z", 0, 0, tiled=True)
    (qkv_grad,) = call(final_kernel, [((held, 3 * width // slabs), f32)], [share], 0, 8)
    return (input_grad[None], qkv_grad)


def solution(mesh):
    split = Mesh(mesh.devices.reshape(SIZES), AXES)
    in_specs = (
        P(DP, TM, None, None),
        P(),
        P(),
        P(),
        P(None, DP, None),
        P(DP, TM, None, None),
    )
    out_specs = (P(DP, TM, None, None), P(DP, TM))

    return jax.shard_map(
        on_device, mesh=split, in_specs=in_specs, out_specs=out_specs, check_vma=False
    )
```

```python
import math

import jax
import jax.numpy as jnp
from jax import lax
from jax.experimental import pallas as pl
from jax.experimental.pallas import tpu as pltpu
from jax.sharding import Mesh
from jax.sharding import PartitionSpec as P

AXES = ("xh", "z", "y", "xl", "co")
SIZES = (2, 16, 4, 2, 2)
DP = ("xh", "z")
TM = ("y", "xl", "co")
PLANE = ("xh", "y", "xl")
PIECES = 8
TILES = 7
LANES = 128
bf16, f32 = jnp.bfloat16, jnp.float32


def dot(a, b, contract):
    return lax.dot_general(a, b, (contract, ((), ())), preferred_element_type=f32)


NN, NT, TN = ((1,), (0,)), ((1,), (1,)), ((0,), (0,))


def forward_kernel(
    clip_ref, gain_ref, weight_ref, order_ref, out_weight_ref, next_any,
    normed_ref, qkv_ref, prob_ref, out_order_ref, next_ref, sem,
):
    frames, _, width = clip_ref.shape
    copy = pltpu.make_async_copy(next_any, next_ref, sem)
    copy.start()
    out_order_ref[...] = dot(out_weight_ref[...], order_ref[...], NT).astype(bf16)
    for f in range(frames):
        features = clip_ref[f].astype(f32)
        squares = jnp.mean(features * features, axis=-1, keepdims=True)
        normed = (features * lax.rsqrt(squares + 1e-06) * gain_ref[...]).astype(bf16)
        normed_ref[f] = normed
        qkv = dot(normed, weight_ref[...], NN).astype(bf16)
        qkv_ref[f] = qkv
        scores = dot(qkv[:, :width], qkv[:, width : 2 * width], NT) / math.sqrt(width)
        raised = jnp.exp(scores - jnp.max(scores, axis=-1, keepdims=True))
        prob_ref[f] = raised / jnp.sum(raised, axis=-1, keepdims=True)
    copy.wait()


def backward_kernel(
    core_ref, cot_ref, next_ref, own_ref, other_ref, order_ref, out_weight_ref, qkv_ref, prob_ref,
    normed_ref, upstream_ref, qkv_cot_ref, keep_ref, send_ref, grad_ref,
):
    frames, positions, width = upstream_ref.shape
    rows = frames * positions
    wide = cot_ref.shape[-1]
    block = own_ref.shape[2]
    groups = own_ref.shape[0] // PIECES
    lanes = wide // LANES
    parts = width // (2 * groups * block)

    def taps_of(tap):
        columns = []
        for lane in range(lanes):
            column = []
            for source in (own_ref, other_ref):
                for group in range(groups):
                    for part in range(parts):
                        tile = (tap * lanes + lane) * parts + part
                        column.append(source[group * PIECES + tile // TILES, tile % TILES])
            columns.append(jnp.concatenate(column, axis=0))
        return columns

    middle = jnp.concatenate([cot_ref[1], next_ref[0]], axis=0)
    seen = [cot_ref[...].reshape(rows, wide), middle, next_ref[...].reshape(rows, wide)]
    taps = jnp.concatenate(taps_of(2) + taps_of(1) + taps_of(0), axis=1)
    total = dot(jnp.concatenate(seen, axis=1), taps, NT)
    arrived = total.astype(bf16)
    mixed_cot = dot(arrived, out_weight_ref[...], NT).astype(bf16)
    cots = [mixed_cot[f * positions : (f + 1) * positions] for f in range(frames)]
    weights_cots = [
        dot(cots[f], qkv_ref[f, :, 2 * width :], NT).astype(bf16).astype(f32)
        for f in range(frames)
    ]
    for f in range(frames):
        qkv_cot_ref[f, :, 2 * width :] = dot(prob_ref[f].astype(bf16), cots[f], TN).astype(bf16)
    scores_cots = []
    for f in range(frames):
        prob = prob_ref[f]
        pull = jnp.sum(weights_cots[f] * prob, axis=-1, keepdims=True)
        scores_cots.append((prob * (weights_cots[f] - pull) / math.sqrt(width)).astype(bf16))
    normed = normed_ref[...].reshape(rows, width)

    for f in range(frames):
        qkv_cot_ref[f, :, :width] = dot(
            scores_cots[f], qkv_ref[f, :, width : 2 * width], NN
        ).astype(bf16)
    for f in range(frames):
        qkv_cot_ref[f, :, width : 2 * width] = dot(
            scores_cots[f], qkv_ref[f, :, :width], TN
        ).astype(bf16)
    upstream_ref[...] = dot(arrived, order_ref[...], NN).astype(bf16).reshape(upstream_ref.shape)
    grad_ref[...] = dot(qkv_cot_ref[...].reshape(rows, 3 * width), normed, TN)
    columns = grad_ref.shape[0] // (2 * PIECES)
    short = keep_ref.shape[1] - columns
    left = lax.broadcasted_iota(jnp.int32, (short, LANES), 1) < LANES // 2
    for out_ref, core in ((keep_ref, core_ref[0]), (send_ref, 1 - core_ref[0])):
        for group in range(groups):
            for chip in range(PIECES):
                top = pl.multiple_of((2 * chip + core) * columns, 8)
                low = pl.multiple_of(top + columns - short, 8)
                upper = grad_ref[pl.ds(top, short), LANES : 2 * LANES]
                lower = grad_ref[pl.ds(low, short), LANES : 2 * LANES]
                if group == 0:
                    lower = pltpu.roll(lower, LANES // 2, 1)
                else:
                    upper = pltpu.roll(upper, LANES // 2, 1)
                side = 2 * group * LANES
                wide_part = grad_ref[pl.ds(top, columns), side : side + LANES]
                out_ref[group * PIECES + chip] = jnp.concatenate(
                    [wide_part, jnp.where(left, upper, lower)], axis=0
                ).astype(bf16)


def turn_kernel(got_ref, turn_ref, out_ref):
    columns, short = 72, got_ref.shape[1] - 72
    depth = out_ref.shape[0]
    total = got_ref[0].astype(f32)
    for i in range(1, got_ref.shape[0]):
        total = total + got_ref[i].astype(f32)
    narrow = total[columns:]
    other = pltpu.roll(narrow, LANES // 2, 1)
    empty = jnp.zeros((LANES - columns, LANES), f32)
    narrow = jnp.concatenate([narrow, other[2 * short - columns :], empty], axis=0)
    wide = jnp.concatenate([total[:columns], empty], axis=0)
    turned = dot(turn_ref[0], wide.astype(bf16), NT) + dot(turn_ref[1], narrow.astype(bf16), NT)
    first, last = turned[: depth * 8], turned[depth * 8 :]
    row = lax.broadcasted_iota(jnp.int32, first.shape, 0)
    lane = lax.broadcasted_iota(jnp.int32, first.shape, 1)
    last = jnp.where(
        lax.rem(row, 2) == 0, pltpu.roll(last, columns, 1), pltpu.roll(last, columns // 2, 1)
    )
    turned = jnp.where(lane < columns, first, last)
    out_ref[...] = turned.astype(bf16).reshape(out_ref.shape)


def final_kernel(got_ref, out_ref):
    columns = out_ref.shape[1]
    total = got_ref[0].astype(f32)
    for i in range(1, got_ref.shape[0]):
        total = total + got_ref[i].astype(f32)
    out_ref[0:8] = total[:, :columns]
    even = pltpu.roll(total, LANES - columns, 1)
    odd = pltpu.roll(total, LANES - columns // 2, 1)
    left = lax.broadcasted_iota(jnp.int32, (1, LANES), 1) < columns // 2
    for i in range(4):
        line = jnp.where(left, even[2 * i : 2 * i + 1], odd[2 * i + 1 : 2 * i + 2])
        out_ref[8 + i : 9 + i] = line[:, :columns]


def input_kernel(clip_ref, gain_ref, weight_ref, qkv_cot_ref, upstream_ref, out_ref):
    frames, _, _ = clip_ref.shape
    for f in range(frames):
        features = clip_ref[f].astype(f32)
        squares = jnp.mean(features * features, axis=-1, keepdims=True)
        scale = lax.rsqrt(squares + 1e-06)
        cot = dot(qkv_cot_ref[f], weight_ref[...], NT) * gain_ref[...]
        along = jnp.mean(features * cot, axis=-1, keepdims=True)
        direct = scale * cot - features * (scale * scale * scale * along)
        out_ref[f] = (upstream_ref[f].astype(f32) + direct).astype(bf16)


def whole(count):
    return [pl.BlockSpec(memory_space=pltpu.VMEM)] * count


def call(kernel, outs, args, flops, limit, scratch=(), specs=None):
    moved = sum(a.size * a.dtype.itemsize for a in args)
    moved += sum(math.prod(s) * jnp.dtype(d).itemsize for s, d in outs)
    return pl.pallas_call(
        kernel,
        out_shape=tuple(jax.ShapeDtypeStruct(s, d) for s, d in outs),
        in_specs=specs or whole(len(args)),
        out_specs=tuple(whole(len(outs))),
        scratch_shapes=list(scratch),
        cost_estimate=pl.CostEstimate(flops=flops, bytes_accessed=moved, transcendentals=0),
        compiler_params=pltpu.CompilerParams(vmem_limit_bytes=limit << 20),
    )(*args)


def spread(block, axes):
    count = math.prod(lax.axis_size(a) for a in axes)
    return lax.all_to_all(
        jnp.broadcast_to(block[None], (count,) + block.shape), axes, 0, 0, tiled=True
    )


def piece_kernel(place_ref, shard_ref, out_ref, tiles_ref):
    taps, held, wide = shard_ref.shape
    lanes, parts = wide // LANES, held // 4
    count = taps * lanes * parts
    slots = PIECES * TILES
    for side in range(2):
        for tile in range(count):
            tap, rest = divmod(tile, lanes * parts)
            lane, part = divmod(rest, parts)
            row = side * held // 2 + 2 * part
            tiles_ref[side * slots + tile] = shard_ref[
                tap, row : row + 2, lane * LANES : (lane + 1) * LANES
            ]
        for tile in range(count, slots):
            tiles_ref[side * slots + tile] = jnp.zeros((2, LANES), bf16)
    piece = tiles_ref[pl.ds(place_ref[0] * TILES, TILES)]
    for i in range(out_ref.shape[0]):
        out_ref[i] = piece


def tap_column(shard, core, group):
    place = lax.axis_index("y") * lax.axis_size("xl") + lax.axis_index("xl") + core * PIECES
    (piece,) = call(
        piece_kernel,
        [((lax.axis_size("z"), TILES, 2, LANES), bf16)],
        [place.reshape(1), shard],
        0,
        8,
        [pltpu.VMEM((2 * PIECES * TILES, 2, LANES), bf16)],
        [pl.BlockSpec(memory_space=pltpu.SMEM)] + whole(1),
    )
    piece, core, group = lax.optimization_barrier((piece, core, group))
    column = lax.all_to_all(piece, ("z",), 0, 0, tiled=True)
    return column.transpose(1, 0, 2, 3).reshape(TILES, -1, LANES), core, group


def channel_order(width, core):
    depth, groups = lax.axis_size("z"), lax.axis_size("xh")
    held = width // (depth * groups)
    parts = held // 4
    place = jnp.arange(width)
    row, place = place % 2, place // 2
    level, place = place % depth, place // depth
    part, place = place % parts, place // parts
    group, half = place % groups, place // groups
    side = jnp.where(core == 0, half, 1 - half)
    channel = held * (group * depth + level) + (held // 2) * side + 2 * part + row
    return (channel[:, None] == jnp.arange(width)[None, :]).astype(bf16)


def turn_orders(held, depth, group):
    row = jnp.arange(depth * 8)
    first = row // 8 * held + row % 8
    last = row // 8 * held + 8 + row % 8 // 2
    channel = jnp.concatenate([first, last])[:, None]
    lane = jnp.arange(LANES)[None, :]
    wide = channel == lane + 64 * group
    narrow = (channel == lane + LANES * (1 - group)) & (lane < 64)
    return jnp.stack([wide, narrow]).astype(bf16)


def on_device(clip_input, norm_gain, qkv_weight, out_weight, time_weight, upsample_cotangent):
    clip = clip_input[0]
    cotangent = upsample_cotangent[0]
    frames, positions, width = clip.shape
    wide = cotangent.shape[-1]
    rows = frames * positions
    slabs = math.prod(lax.axis_size(a) for a in TM)
    clips = math.prod(lax.axis_size(a) for a in DP)
    gain = norm_gain[None]

    depth = lax.axis_size("z")
    held = width // clips
    swap = [(0, 1), (1, 0)]
    incoming = lax.ppermute(cotangent, TM, [(i + 1, i) for i in range(slabs - 1)])
    column, core, group = tap_column(
        time_weight, lax.axis_index("co"), lax.axis_index("xh")
    )
    column, core, group = lax.optimization_barrier((column, core, group))
    own = spread(column, PLANE)
    own, clip, core, group = lax.optimization_barrier((own, clip, core, group))
    other = lax.ppermute(own, "co", swap)
    order = channel_order(width, core)
    normed, qkv, prob, out_order, following = call(
        forward_kernel,
        [((frames, positions, width), bf16), ((frames, positions, 3 * width), bf16),
         ((frames, positions, positions), f32), ((width, width), bf16), (incoming.shape, bf16)],
        [clip, gain, qkv_weight, order, out_weight,
         pltpu.with_memory_space_constraint(incoming, pltpu.HBM)],
        2 * rows * width * (3 * width + positions),
        16,
        [pltpu.SemaphoreType.DMA],
        whole(5) + [pl.BlockSpec(memory_space=pl.ANY)],
    )
    turn = turn_orders(held, depth, group)
    core = core.reshape(1)

    chips = own.shape[0]
    packed = ((chips, 112, LANES), bf16)
    upstream, qkv_cot, keep, send = call(
        backward_kernel,
        [((frames, positions, width), bf16), ((frames, positions, 3 * width), bf16), packed, packed],
        [core, cotangent, following, own, other, order, out_order, qkv, prob, normed],
        2 * rows * width * (3 * wide + 2 * width + 4 * positions + 3 * width),
        32,
        [pltpu.VMEM((3 * width, width), f32)],
        [pl.BlockSpec(memory_space=pltpu.SMEM)] + whole(9),
    )
    got = lax.ppermute(send, "co", swap)
    (input_grad,) = call(
        input_kernel,
        [((frames, positions, width), bf16)],
        [clip, gain, qkv_weight, qkv_cot, upstream],
        2 * rows * width * 3 * width,
        16,
    )
    got, input_grad, turn = lax.optimization_barrier((got, input_grad, turn))
    share = (keep.astype(f32) + got.astype(f32)).astype(bf16)
    share = lax.all_to_all(share, PLANE, 0, 0, tiled=True)
    (share,) = call(
        turn_kernel,
        [((depth, 8, LANES), bf16)],
        [share, turn],
        2 * depth * 16 * 72 * 2 * LANES,
        16,
    )
    share = lax.all_to_all(share, "z", 0, 0, tiled=True)
    (qkv_grad,) = call(final_kernel, [((held, 3 * width // slabs), f32)], [share], 0, 8)
    return (input_grad[None], qkv_grad)


def solution(mesh):
    split = Mesh(mesh.devices.reshape(SIZES), AXES)
    in_specs = (
        P(DP, TM, None, None),
        P(),
        P(),
        P(),
        P(None, DP, None),
        P(DP, TM, None, None),
    )
    out_specs = (P(DP, TM, None, None), P(DP, TM))

    return jax.shard_map(
        on_device, mesh=split, in_specs=in_specs, out_specs=out_specs, check_vma=False
    )
```

```python
import math

import jax
import jax.numpy as jnp
from jax import lax
from jax.experimental import pallas as pl
from jax.experimental.pallas import tpu as pltpu
from jax.sharding import Mesh
from jax.sharding import PartitionSpec as P

AXES = ("xh", "z", "y", "xl", "co")
SIZES = (2, 16, 4, 2, 2)
DP = ("xh", "z")
TM = ("y", "xl", "co")
PLANE = ("xh", "y", "xl")
PIECES = 8
TILES = 7
LANES = 128
bf16, f32 = jnp.bfloat16, jnp.float32


def dot(a, b, contract):
    return lax.dot_general(a, b, (contract, ((), ())), preferred_element_type=f32)


NN, NT, TN = ((1,), (0,)), ((1,), (1,)), ((0,), (0,))


def forward_kernel(
    clip_ref, gain_ref, weight_ref, order_ref, out_weight_ref, next_any,
    normed_ref, qkv_ref, prob_ref, out_order_ref, next_ref, sem,
):
    frames, _, width = clip_ref.shape
    copy = pltpu.make_async_copy(next_any, next_ref, sem)
    copy.start()
    out_order_ref[...] = dot(out_weight_ref[...], order_ref[...], NT).astype(bf16)
    for f in range(frames):
        features = clip_ref[f].astype(f32)
        squares = jnp.mean(features * features, axis=-1, keepdims=True)
        normed = (features * lax.rsqrt(squares + 1e-06) * gain_ref[...]).astype(bf16)
        normed_ref[f] = normed
        qkv = dot(normed, weight_ref[...], NN).astype(bf16)
        qkv_ref[f] = qkv
        scores = dot(qkv[:, :width], qkv[:, width : 2 * width], NT) / math.sqrt(width)
        raised = jnp.exp(scores - jnp.max(scores, axis=-1, keepdims=True))
        prob_ref[f] = raised / jnp.sum(raised, axis=-1, keepdims=True)
    copy.wait()


def backward_kernel(
    core_ref, cot_ref, next_ref, own_ref, other_ref, order_ref, out_weight_ref, qkv_ref, prob_ref,
    normed_ref, upstream_ref, qkv_cot_ref, keep_ref, send_ref, grad_ref,
):
    frames, positions, width = upstream_ref.shape
    rows = frames * positions
    wide = cot_ref.shape[-1]
    block = own_ref.shape[2]
    groups = own_ref.shape[0] // PIECES
    lanes = wide // LANES
    parts = width // (2 * groups * block)

    def taps_of(tap):
        columns = []
        for lane in range(lanes):
            column = []
            for source in (own_ref, other_ref):
                for group in range(groups):
                    for part in range(parts):
                        tile = (tap * lanes + lane) * parts + part
                        column.append(source[group * PIECES + tile // TILES, tile % TILES])
            columns.append(jnp.concatenate(column, axis=0))
        return columns

    middle = jnp.concatenate([cot_ref[1], next_ref[0]], axis=0)
    seen = [cot_ref[...].reshape(rows, wide), middle, next_ref[...].reshape(rows, wide)]
    taps = jnp.concatenate(taps_of(2) + taps_of(1) + taps_of(0), axis=1)
    total = dot(jnp.concatenate(seen, axis=1), taps, NT)
    arrived = total.astype(bf16)
    mixed_cot = dot(arrived, out_weight_ref[...], NT).astype(bf16)
    cots = [mixed_cot[f * positions : (f + 1) * positions] for f in range(frames)]
    weights_cots = [
        dot(cots[f], qkv_ref[f, :, 2 * width :], NT).astype(bf16).astype(f32)
        for f in range(frames)
    ]
    for f in range(frames):
        qkv_cot_ref[f, :, 2 * width :] = dot(prob_ref[f].astype(bf16), cots[f], TN).astype(bf16)
    scores_cots = []
    for f in range(frames):
        prob = prob_ref[f]
        pull = jnp.sum(weights_cots[f] * prob, axis=-1, keepdims=True)
        scores_cots.append((prob * (weights_cots[f] - pull) / math.sqrt(width)).astype(bf16))
    normed = normed_ref[...].reshape(rows, width)

    for f in range(frames):
        qkv_cot_ref[f, :, :width] = dot(
            scores_cots[f], qkv_ref[f, :, width : 2 * width], NN
        ).astype(bf16)
    for f in range(frames):
        qkv_cot_ref[f, :, width : 2 * width] = dot(
            scores_cots[f], qkv_ref[f, :, :width], TN
        ).astype(bf16)
    upstream_ref[...] = dot(arrived, order_ref[...], NN).astype(bf16).reshape(upstream_ref.shape)
    grad_ref[...] = dot(qkv_cot_ref[...].reshape(rows, 3 * width), normed, TN)
    columns = grad_ref.shape[0] // (2 * PIECES)
    short = keep_ref.shape[1] - columns
    left = lax.broadcasted_iota(jnp.int32, (short, LANES), 1) < LANES // 2
    for out_ref, core in ((keep_ref, core_ref[0]), (send_ref, 1 - core_ref[0])):
        for group in range(groups):
            for chip in range(PIECES):
                top = pl.multiple_of((2 * chip + core) * columns, 8)
                low = pl.multiple_of(top + columns - short, 8)
                upper = grad_ref[pl.ds(top, short), LANES : 2 * LANES]
                lower = grad_ref[pl.ds(low, short), LANES : 2 * LANES]
                if group == 0:
                    lower = pltpu.roll(lower, LANES // 2, 1)
                else:
                    upper = pltpu.roll(upper, LANES // 2, 1)
                side = 2 * group * LANES
                wide_part = grad_ref[pl.ds(top, columns), side : side + LANES]
                out_ref[group * PIECES + chip] = jnp.concatenate(
                    [wide_part, jnp.where(left, upper, lower)], axis=0
                ).astype(bf16)


def turn_kernel(got_ref, turn_ref, out_ref):
    columns, short = 72, got_ref.shape[1] - 72
    depth = out_ref.shape[0]
    total = got_ref[0].astype(f32)
    for i in range(1, got_ref.shape[0]):
        total = total + got_ref[i].astype(f32)
    narrow = total[columns:]
    other = pltpu.roll(narrow, LANES // 2, 1)
    empty = jnp.zeros((LANES - columns, LANES), f32)
    narrow = jnp.concatenate([narrow, other[2 * short - columns :], empty], axis=0)
    wide = jnp.concatenate([total[:columns], empty], axis=0)
    turned = dot(turn_ref[0], wide.astype(bf16), NT) + dot(turn_ref[1], narrow.astype(bf16), NT)
    first, last = turned[: depth * 8], turned[depth * 8 :]
    row = lax.broadcasted_iota(jnp.int32, first.shape, 0)
    lane = lax.broadcasted_iota(jnp.int32, first.shape, 1)
    last = jnp.where(
        lax.rem(row, 2) == 0, pltpu.roll(last, columns, 1), pltpu.roll(last, columns // 2, 1)
    )
    turned = jnp.where(lane < columns, first, last)
    out_ref[...] = turned.astype(bf16).reshape(out_ref.shape)


def final_kernel(got_ref, out_ref):
    columns = out_ref.shape[1]
    total = got_ref[0].astype(f32)
    for i in range(1, got_ref.shape[0]):
        total = total + got_ref[i].astype(f32)
    out_ref[0:8] = total[:, :columns]
    even = pltpu.roll(total, LANES - columns, 1)
    odd = pltpu.roll(total, LANES - columns // 2, 1)
    left = lax.broadcasted_iota(jnp.int32, (1, LANES), 1) < columns // 2
    for i in range(4):
        line = jnp.where(left, even[2 * i : 2 * i + 1], odd[2 * i + 1 : 2 * i + 2])
        out_ref[8 + i : 9 + i] = line[:, :columns]


def input_kernel(
    clip_ref, gain_ref, weight_ref, qkv_cot_ref, upstream_ref, out_any, out_ref, sems
):
    frames, _, _ = clip_ref.shape
    copies = []
    for f in range(frames):
        features = clip_ref[f].astype(f32)
        squares = jnp.mean(features * features, axis=-1, keepdims=True)
        scale = lax.rsqrt(squares + 1e-06)
        cot = dot(qkv_cot_ref[f], weight_ref[...], NT) * gain_ref[...]
        along = jnp.mean(features * cot, axis=-1, keepdims=True)
        direct = scale * cot - features * (scale * scale * scale * along)
        out_ref[f] = (upstream_ref[f].astype(f32) + direct).astype(bf16)
        copies.append(pltpu.make_async_copy(out_ref.at[f], out_any.at[f], sems.at[f]))
        copies[f].start()
    for copy in copies:
        copy.wait()


def whole(count):
    return [pl.BlockSpec(memory_space=pltpu.VMEM)] * count


def call(kernel, outs, args, flops, limit, scratch=(), specs=None, out_specs=None):
    moved = sum(a.size * a.dtype.itemsize for a in args)
    moved += sum(math.prod(s) * jnp.dtype(d).itemsize for s, d in outs)
    return pl.pallas_call(
        kernel,
        out_shape=tuple(jax.ShapeDtypeStruct(s, d) for s, d in outs),
        in_specs=specs or whole(len(args)),
        out_specs=tuple(out_specs or whole(len(outs))),
        scratch_shapes=list(scratch),
        cost_estimate=pl.CostEstimate(flops=flops, bytes_accessed=moved, transcendentals=0),
        compiler_params=pltpu.CompilerParams(vmem_limit_bytes=limit << 20),
    )(*args)


def spread(block, axes):
    count = math.prod(lax.axis_size(a) for a in axes)
    return lax.all_to_all(
        jnp.broadcast_to(block[None], (count,) + block.shape), axes, 0, 0, tiled=True
    )


def piece_kernel(place_ref, shard_any, out_ref, tiles_ref, shard_ref, sem):
    copy = pltpu.make_async_copy(shard_any, shard_ref, sem)
    copy.start()
    copy.wait()
    taps, held, wide = shard_ref.shape
    lanes, parts = wide // LANES, held // 4
    count = taps * lanes * parts
    slots = PIECES * TILES
    for side in range(2):
        for tile in range(count):
            tap, rest = divmod(tile, lanes * parts)
            lane, part = divmod(rest, parts)
            row = side * held // 2 + 2 * part
            tiles_ref[side * slots + tile] = shard_ref[
                tap, row : row + 2, lane * LANES : (lane + 1) * LANES
            ]
        for tile in range(count, slots):
            tiles_ref[side * slots + tile] = jnp.zeros((2, LANES), bf16)
    piece = tiles_ref[pl.ds(place_ref[0] * TILES, TILES)]
    for i in range(out_ref.shape[0]):
        out_ref[i] = piece


def tap_column(shard, core, group):
    place = lax.axis_index("y") * lax.axis_size("xl") + lax.axis_index("xl") + core * PIECES
    (piece,) = call(
        piece_kernel,
        [((lax.axis_size("z"), TILES, 2, LANES), bf16)],
        [place.reshape(1), pltpu.with_memory_space_constraint(shard, pltpu.HBM)],
        0,
        8,
        [pltpu.VMEM((2 * PIECES * TILES, 2, LANES), bf16), pltpu.VMEM(shard.shape, bf16),
         pltpu.SemaphoreType.DMA],
        [pl.BlockSpec(memory_space=pltpu.SMEM), pl.BlockSpec(memory_space=pl.ANY)],
    )
    piece, core, group = lax.optimization_barrier((piece, core, group))
    column = lax.all_to_all(piece, ("z",), 0, 0, tiled=True)
    return column.transpose(1, 0, 2, 3).reshape(TILES, -1, LANES), core, group


def channel_order(width, core):
    depth, groups = lax.axis_size("z"), lax.axis_size("xh")
    held = width // (depth * groups)
    parts = held // 4
    place = jnp.arange(width)
    row, place = place % 2, place // 2
    level, place = place % depth, place // depth
    part, place = place % parts, place // parts
    group, half = place % groups, place // groups
    side = jnp.where(core == 0, half, 1 - half)
    channel = held * (group * depth + level) + (held // 2) * side + 2 * part + row
    return (channel[:, None] == jnp.arange(width)[None, :]).astype(bf16)


def turn_orders(held, depth, group):
    row = jnp.arange(depth * 8)
    first = row // 8 * held + row % 8
    last = row // 8 * held + 8 + row % 8 // 2
    channel = jnp.concatenate([first, last])[:, None]
    lane = jnp.arange(LANES)[None, :]
    wide = channel == lane + 64 * group
    narrow = (channel == lane + LANES * (1 - group)) & (lane < 64)
    return jnp.stack([wide, narrow]).astype(bf16)


def on_device(clip_input, norm_gain, qkv_weight, out_weight, time_weight, upsample_cotangent):
    clip = clip_input[0]
    cotangent = upsample_cotangent[0]
    frames, positions, width = clip.shape
    wide = cotangent.shape[-1]
    rows = frames * positions
    slabs = math.prod(lax.axis_size(a) for a in TM)
    clips = math.prod(lax.axis_size(a) for a in DP)
    gain = norm_gain[None]

    depth = lax.axis_size("z")
    held = width // clips
    swap = [(0, 1), (1, 0)]
    incoming = lax.ppermute(cotangent, TM, [(i + 1, i) for i in range(slabs - 1)])
    column, core, group = tap_column(
        time_weight, lax.axis_index("co"), lax.axis_index("xh")
    )
    column, core, group = lax.optimization_barrier((column, core, group))
    own = spread(column, PLANE)
    own, clip, core, group = lax.optimization_barrier((own, clip, core, group))
    other = lax.ppermute(own, "co", swap)
    order = channel_order(width, core)
    normed, qkv, prob, out_order, following = call(
        forward_kernel,
        [((frames, positions, width), bf16), ((frames, positions, 3 * width), bf16),
         ((frames, positions, positions), f32), ((width, width), bf16), (incoming.shape, bf16)],
        [clip, gain, qkv_weight, order, out_weight,
         pltpu.with_memory_space_constraint(incoming, pltpu.HBM)],
        2 * rows * width * (3 * width + positions),
        16,
        [pltpu.SemaphoreType.DMA],
        whole(5) + [pl.BlockSpec(memory_space=pl.ANY)],
    )
    turn = turn_orders(held, depth, group)
    core = core.reshape(1)

    chips = own.shape[0]
    packed = ((chips, 112, LANES), bf16)
    upstream, qkv_cot, keep, send = call(
        backward_kernel,
        [((frames, positions, width), bf16), ((frames, positions, 3 * width), bf16), packed, packed],
        [core, cotangent, following, own, other, order, out_order, qkv, prob, normed],
        2 * rows * width * (3 * wide + 2 * width + 4 * positions + 3 * width),
        32,
        [pltpu.VMEM((3 * width, width), f32)],
        [pl.BlockSpec(memory_space=pltpu.SMEM)] + whole(9),
    )
    got = lax.ppermute(send, "co", swap)
    (input_grad,) = call(
        input_kernel,
        [((frames, positions, width), bf16)],
        [clip, gain, qkv_weight, qkv_cot, upstream],
        2 * rows * width * 3 * width,
        16,
        [pltpu.VMEM(clip.shape, bf16), pltpu.SemaphoreType.DMA((2,))],
        None,
        [pl.BlockSpec(memory_space=pl.ANY)],
    )
    got, input_grad, turn = lax.optimization_barrier((got, input_grad, turn))
    share = (keep.astype(f32) + got.astype(f32)).astype(bf16)
    share = lax.all_to_all(share, PLANE, 0, 0, tiled=True)
    (share,) = call(
        turn_kernel,
        [((depth, 8, LANES), bf16)],
        [share, turn],
        2 * depth * 16 * 72 * 2 * LANES,
        16,
    )
    share = lax.all_to_all(share, "z", 0, 0, tiled=True)
    (qkv_grad,) = call(final_kernel, [((held, 3 * width // slabs), f32)], [share], 0, 8)
    return (input_grad[None], qkv_grad)


def solution(mesh):
    split = Mesh(mesh.devices.reshape(SIZES), AXES)
    in_specs = (
        P(DP, TM, None, None),
        P(),
        P(),
        P(),
        P(None, DP, None),
        P(DP, TM, None, None),
    )
    out_specs = (P(DP, TM, None, None), P(DP, TM))

    return jax.shard_map(
        on_device, mesh=split, in_specs=in_specs, out_specs=out_specs, check_vma=False
    )
```

```python
import math

import jax
import jax.numpy as jnp
from jax import lax
from jax.experimental import pallas as pl
from jax.experimental.pallas import tpu as pltpu
from jax.sharding import Mesh
from jax.sharding import PartitionSpec as P

AXES = ("xh", "z", "y", "xl", "co")
SIZES = (2, 16, 4, 2, 2)
DP = ("xh", "z")
TM = ("y", "xl", "co")
PLANE = ("xh", "y", "xl")
PIECES = 8
TILES = 7
LANES = 128
bf16, f32 = jnp.bfloat16, jnp.float32


def dot(a, b, contract):
    return lax.dot_general(a, b, (contract, ((), ())), preferred_element_type=f32)


NN, NT, TN = ((1,), (0,)), ((1,), (1,)), ((0,), (0,))


def forward_kernel(
    clip_ref, gain_ref, weight_ref, order_ref, out_weight_ref, next_any,
    normed_ref, qkv_ref, prob_ref, out_order_ref, next_ref, sem,
):
    frames, _, width = clip_ref.shape
    copy = pltpu.make_async_copy(next_any, next_ref, sem)
    copy.start()
    out_order_ref[...] = dot(out_weight_ref[...], order_ref[...], NT).astype(bf16)
    for f in range(frames):
        features = clip_ref[f].astype(f32)
        squares = jnp.mean(features * features, axis=-1, keepdims=True)
        normed = (features * lax.rsqrt(squares + 1e-06) * gain_ref[...]).astype(bf16)
        normed_ref[f] = normed
        qkv = dot(normed, weight_ref[...], NN).astype(bf16)
        qkv_ref[f] = qkv
        scores = dot(qkv[:, :width], qkv[:, width : 2 * width], NT) / math.sqrt(width)
        raised = jnp.exp(scores - jnp.max(scores, axis=-1, keepdims=True))
        prob_ref[f] = raised / jnp.sum(raised, axis=-1, keepdims=True)
    copy.wait()


def backward_kernel(
    core_ref, cot_ref, next_ref, own_ref, other_ref, order_ref, out_weight_ref, qkv_ref, prob_ref,
    normed_ref, upstream_ref, qkv_cot_ref, keep_ref, send_ref, grad_ref,
):
    frames, positions, width = upstream_ref.shape
    rows = frames * positions
    wide = cot_ref.shape[-1]
    block = own_ref.shape[2]
    groups = own_ref.shape[0] // PIECES
    lanes = wide // LANES
    parts = width // (2 * groups * block)

    def taps_of(tap):
        columns = []
        for lane in range(lanes):
            column = []
            for source in (own_ref, other_ref):
                for group in range(groups):
                    for part in range(parts):
                        tile = (tap * lanes + lane) * parts + part
                        column.append(source[group * PIECES + tile // TILES, tile % TILES])
            columns.append(jnp.concatenate(column, axis=0))
        return columns

    middle = jnp.concatenate([cot_ref[1], next_ref[0]], axis=0)
    seen = [cot_ref[...].reshape(rows, wide), middle, next_ref[...].reshape(rows, wide)]
    taps = jnp.concatenate(taps_of(2) + taps_of(1) + taps_of(0), axis=1)
    total = dot(jnp.concatenate(seen, axis=1), taps, NT)
    arrived = total.astype(bf16)
    mixed_cot = dot(arrived, out_weight_ref[...], NT).astype(bf16)
    cots = [mixed_cot[f * positions : (f + 1) * positions] for f in range(frames)]
    weights_cots = [
        dot(cots[f], qkv_ref[f, :, 2 * width :], NT).astype(bf16).astype(f32)
        for f in range(frames)
    ]
    for f in range(frames):
        qkv_cot_ref[f, :, 2 * width :] = dot(prob_ref[f].astype(bf16), cots[f], TN).astype(bf16)
    scores_cots = []
    for f in range(frames):
        prob = prob_ref[f]
        pull = jnp.sum(weights_cots[f] * prob, axis=-1, keepdims=True)
        scores_cots.append((prob * (weights_cots[f] - pull) / math.sqrt(width)).astype(bf16))
    normed = normed_ref[...].reshape(rows, width)

    for f in range(frames):
        qkv_cot_ref[f, :, :width] = dot(
            scores_cots[f], qkv_ref[f, :, width : 2 * width], NN
        ).astype(bf16)
    for f in range(frames):
        qkv_cot_ref[f, :, width : 2 * width] = dot(
            scores_cots[f], qkv_ref[f, :, :width], TN
        ).astype(bf16)
    upstream_ref[...] = dot(arrived, order_ref[...], NN).astype(bf16).reshape(upstream_ref.shape)
    grad_ref[...] = dot(qkv_cot_ref[...].reshape(rows, 3 * width), normed, TN)
    columns = grad_ref.shape[0] // (2 * PIECES)
    short = keep_ref.shape[1] - columns
    left = lax.broadcasted_iota(jnp.int32, (short, LANES), 1) < LANES // 2
    for out_ref, core in ((keep_ref, core_ref[0]), (send_ref, 1 - core_ref[0])):
        for group in range(groups):
            for chip in range(PIECES):
                top = pl.multiple_of((2 * chip + core) * columns, 8)
                low = pl.multiple_of(top + columns - short, 8)
                upper = grad_ref[pl.ds(top, short), LANES : 2 * LANES]
                lower = grad_ref[pl.ds(low, short), LANES : 2 * LANES]
                if group == 0:
                    lower = pltpu.roll(lower, LANES // 2, 1)
                else:
                    upper = pltpu.roll(upper, LANES // 2, 1)
                side = 2 * group * LANES
                wide_part = grad_ref[pl.ds(top, columns), side : side + LANES]
                out_ref[groups * chip + group] = jnp.concatenate(
                    [wide_part, jnp.where(left, upper, lower)], axis=0
                ).astype(bf16)


def turn_kernel(got_ref, turn_ref, out_ref):
    columns, short = 72, got_ref.shape[1] - 72
    depth = turn_ref.shape[1] // 16
    groups = out_ref.shape[0] // depth
    for group in range(groups):
        total = got_ref[group].astype(f32)
        for i in range(group + groups, got_ref.shape[0], groups):
            total = total + got_ref[i].astype(f32)
        narrow = total[columns:]
        other = pltpu.roll(narrow, LANES // 2, 1)
        empty = jnp.zeros((LANES - columns, LANES), f32)
        narrow = jnp.concatenate([narrow, other[2 * short - columns :], empty], axis=0)
        wide = jnp.concatenate([total[:columns], empty], axis=0)
        turned = dot(turn_ref[2 * group], wide.astype(bf16), NT)
        turned = turned + dot(turn_ref[2 * group + 1], narrow.astype(bf16), NT)
        first, last = turned[: depth * 8], turned[depth * 8 :]
        row = lax.broadcasted_iota(jnp.int32, first.shape, 0)
        lane = lax.broadcasted_iota(jnp.int32, first.shape, 1)
        last = jnp.where(
            lax.rem(row, 2) == 0, pltpu.roll(last, columns, 1), pltpu.roll(last, columns // 2, 1)
        )
        turned = jnp.where(lane < columns, first, last).astype(bf16)
        out_ref[group * depth : (group + 1) * depth] = turned.reshape(depth, 8, LANES)


def final_kernel(got_ref, out_ref):
    columns = out_ref.shape[1]
    total = got_ref[0].astype(f32)
    for i in range(1, got_ref.shape[0]):
        total = total + got_ref[i].astype(f32)
    out_ref[0:8] = total[:, :columns]
    even = pltpu.roll(total, LANES - columns, 1)
    odd = pltpu.roll(total, LANES - columns // 2, 1)
    left = lax.broadcasted_iota(jnp.int32, (1, LANES), 1) < columns // 2
    for i in range(4):
        line = jnp.where(left, even[2 * i : 2 * i + 1], odd[2 * i + 1 : 2 * i + 2])
        out_ref[8 + i : 9 + i] = line[:, :columns]


def input_kernel(clip_ref, gain_ref, weight_ref, qkv_cot_ref, upstream_ref, out_ref):
    frames, _, _ = clip_ref.shape
    for f in range(frames):
        features = clip_ref[f].astype(f32)
        squares = jnp.mean(features * features, axis=-1, keepdims=True)
        scale = lax.rsqrt(squares + 1e-06)
        cot = dot(qkv_cot_ref[f], weight_ref[...], NT) * gain_ref[...]
        along = jnp.mean(features * cot, axis=-1, keepdims=True)
        direct = scale * cot - features * (scale * scale * scale * along)
        out_ref[f] = (upstream_ref[f].astype(f32) + direct).astype(bf16)


def whole(count):
    return [pl.BlockSpec(memory_space=pltpu.VMEM)] * count


def call(kernel, outs, args, flops, limit, scratch=(), specs=None):
    moved = sum(a.size * a.dtype.itemsize for a in args)
    moved += sum(math.prod(s) * jnp.dtype(d).itemsize for s, d in outs)
    return pl.pallas_call(
        kernel,
        out_shape=tuple(jax.ShapeDtypeStruct(s, d) for s, d in outs),
        in_specs=specs or whole(len(args)),
        out_specs=tuple(whole(len(outs))),
        scratch_shapes=list(scratch),
        cost_estimate=pl.CostEstimate(flops=flops, bytes_accessed=moved, transcendentals=0),
        compiler_params=pltpu.CompilerParams(vmem_limit_bytes=limit << 20),
    )(*args)


def spread(block, axes):
    count = math.prod(lax.axis_size(a) for a in axes)
    return lax.all_to_all(
        jnp.broadcast_to(block[None], (count,) + block.shape), axes, 0, 0, tiled=True
    )


def piece_kernel(place_ref, shard_ref, out_ref, tiles_ref):
    taps, held, wide = shard_ref.shape
    lanes, parts = wide // LANES, held // 4
    count = taps * lanes * parts
    slots = PIECES * TILES
    for side in range(2):
        for tile in range(count):
            tap, rest = divmod(tile, lanes * parts)
            lane, part = divmod(rest, parts)
            row = side * held // 2 + 2 * part
            tiles_ref[side * slots + tile] = shard_ref[
                tap, row : row + 2, lane * LANES : (lane + 1) * LANES
            ]
        for tile in range(count, slots):
            tiles_ref[side * slots + tile] = jnp.zeros((2, LANES), bf16)
    piece = tiles_ref[pl.ds(place_ref[0] * TILES, TILES)]
    for i in range(out_ref.shape[0]):
        out_ref[i] = piece


def tap_column(shard, core, group):
    place = lax.axis_index("y") * lax.axis_size("xl") + lax.axis_index("xl") + core * PIECES
    (piece,) = call(
        piece_kernel,
        [((lax.axis_size("z"), TILES, 2, LANES), bf16)],
        [place.reshape(1), shard],
        0,
        8,
        [pltpu.VMEM((2 * PIECES * TILES, 2, LANES), bf16)],
        [pl.BlockSpec(memory_space=pltpu.SMEM)] + whole(1),
    )
    piece, core, group = lax.optimization_barrier((piece, core, group))
    column = lax.all_to_all(piece, ("z",), 0, 0, tiled=True)
    return column.transpose(1, 0, 2, 3).reshape(TILES, -1, LANES), core, group


def channel_order(width, core):
    depth, groups = lax.axis_size("z"), lax.axis_size("xh")
    held = width // (depth * groups)
    parts = held // 4
    place = jnp.arange(width)
    row, place = place % 2, place // 2
    level, place = place % depth, place // depth
    part, place = place % parts, place // parts
    group, half = place % groups, place // groups
    side = jnp.where(core == 0, half, 1 - half)
    channel = held * (group * depth + level) + (held // 2) * side + 2 * part + row
    return (channel[:, None] == jnp.arange(width)[None, :]).astype(bf16)


def turn_orders(held, depth, group):
    row = jnp.arange(depth * 8)
    first = row // 8 * held + row % 8
    last = row // 8 * held + 8 + row % 8 // 2
    channel = jnp.concatenate([first, last])[:, None]
    lane = jnp.arange(LANES)[None, :]
    wide = channel == lane + 64 * group
    narrow = (channel == lane + LANES * (1 - group)) & (lane < 64)
    return jnp.stack([wide, narrow]).astype(bf16)


def on_device(clip_input, norm_gain, qkv_weight, out_weight, time_weight, upsample_cotangent):
    clip = clip_input[0]
    cotangent = upsample_cotangent[0]
    frames, positions, width = clip.shape
    wide = cotangent.shape[-1]
    rows = frames * positions
    slabs = math.prod(lax.axis_size(a) for a in TM)
    clips = math.prod(lax.axis_size(a) for a in DP)
    gain = norm_gain[None]

    depth = lax.axis_size("z")
    held = width // clips
    swap = [(0, 1), (1, 0)]
    incoming = lax.ppermute(cotangent, TM, [(i + 1, i) for i in range(slabs - 1)])
    column, core, group = tap_column(
        time_weight, lax.axis_index("co"), lax.axis_index("xh")
    )
    column, core, group = lax.optimization_barrier((column, core, group))
    own = spread(column, PLANE)
    own, clip, core, group = lax.optimization_barrier((own, clip, core, group))
    other = lax.ppermute(own, "co", swap)
    order = channel_order(width, core)
    normed, qkv, prob, out_order, following = call(
        forward_kernel,
        [((frames, positions, width), bf16), ((frames, positions, 3 * width), bf16),
         ((frames, positions, positions), f32), ((width, width), bf16), (incoming.shape, bf16)],
        [clip, gain, qkv_weight, order, out_weight,
         pltpu.with_memory_space_constraint(incoming, pltpu.HBM)],
        2 * rows * width * (3 * width + positions),
        16,
        [pltpu.SemaphoreType.DMA],
        whole(5) + [pl.BlockSpec(memory_space=pl.ANY)],
    )
    turn = jnp.concatenate([turn_orders(held, depth, g) for g in range(2)])
    core = core.reshape(1)

    chips = own.shape[0]
    packed = ((chips, 112, LANES), bf16)
    upstream, qkv_cot, keep, send = call(
        backward_kernel,
        [((frames, positions, width), bf16), ((frames, positions, 3 * width), bf16), packed, packed],
        [core, cotangent, following, own, other, order, out_order, qkv, prob, normed],
        2 * rows * width * (3 * wide + 2 * width + 4 * positions + 3 * width),
        32,
        [pltpu.VMEM((3 * width, width), f32)],
        [pl.BlockSpec(memory_space=pltpu.SMEM)] + whole(9),
    )
    got = lax.ppermute(send, "co", swap)
    (input_grad,) = call(
        input_kernel,
        [((frames, positions, width), bf16)],
        [clip, gain, qkv_weight, qkv_cot, upstream],
        2 * rows * width * 3 * width,
        16,
    )
    got, input_grad, turn = lax.optimization_barrier((got, input_grad, turn))
    share = (keep.astype(f32) + got.astype(f32)).astype(bf16)
    share = lax.all_to_all(share, ("y", "xl"), 0, 0, tiled=True)
    (share,) = call(
        turn_kernel,
        [((2 * depth, 8, LANES), bf16)],
        [share, turn],
        2 * depth * 16 * 72 * 2 * LANES,
        16,
    )
    share = lax.all_to_all(share, DP, 0, 0, tiled=True)
    (qkv_grad,) = call(final_kernel, [((held, 3 * width // slabs), f32)], [share], 0, 8)
    return (input_grad[None], qkv_grad)


def solution(mesh):
    split = Mesh(mesh.devices.reshape(SIZES), AXES)
    in_specs = (
        P(DP, TM, None, None),
        P(),
        P(),
        P(),
        P(None, DP, None),
        P(DP, TM, None, None),
    )
    out_specs = (P(DP, TM, None, None), P(DP, TM))

    return jax.shard_map(
        on_device, mesh=split, in_specs=in_specs, out_specs=out_specs, check_vma=False
    )
```
